128 devices in a mesh: dp: 8 (over y, core), prompt: 16 (over x, z).
Axes of the slice: x: 4, y: 4, z: 4, core: 2. Of those that a mesh axis runs over, the one named last changes fastest.
Arguments:
- cand_hidden: bfloat16 [16, 8, 128, 1024], P('prompt', 'dp')
- ref_hidden: bfloat16 [32, 16, 128, 1024], P('dp', 'prompt')
- cand_ids: int32 [16, 8, 128], P('prompt', 'dp'), may hold values from 0 to 50264
- ref_ids: int32 [32, 16, 128], P('dp', 'prompt'), may hold values from 0 to 50264
- cand_len: int32 [16, 8], P('prompt', 'dp'), may hold values from 32 to 128
- reference_length: int32 [32, 16], P('dp', 'prompt'), may hold values from 32 to 128
- idf_table: float32 [50265], replicated, may hold values from 1 to 10
- up_weight: bfloat16 [1024, 4096], replicated, may hold values from -0.1875 to 0.1875
- up_bias: float32 [4096], replicated, may hold values from -3 to 3
- down_weight: bfloat16 [4096, 1024], replicated, may hold values from -0.09375 to 0.09375
- down_bias: float32 [1024], replicated, may hold values from -3 to 3
- norm_gain: float32 [1024], replicated, may hold values from 0.3 to 3
- norm_bias: float32 [1024], replicated, may hold values from -3 to 3
- pair_cand: int32 [8, 16, 32], P('dp', 'prompt'), may hold values from 0 to 7
- pair_ref: int32 [8, 16, 32], P('dp', 'prompt'), may hold values from 0 to 63
- pair_count: int32 [8, 16], P('dp', 'prompt'), may hold values from 8 to 32, as said below
Outputs:
- pair_scores: float32 [3, 8, 16, 32], P(None, 'dp', 'prompt')
- totals: float32 [3], replicated
The draws below stay inside these ranges and needn't reach their ends.
Inputs may be any that keep to these rules, and one draw needn't show every extreme that they name: Slots from pair_count on are not live; some device has all 32 slots live.
All inputs are finite; a program needn't handle non-finite values.
Results may differ from the reference program's by a relative error of at most 0.0003.
Values may be sent and summed in bfloat16 or wider, within the bound.
No kernel may reach another device: no remote copies, remote signals or barrier semaphores. Data moves between devices by JAX's collectives and lax.ppermute only.
A program may use at most 128 MiB of HBM per device.

```python
import math
import jax
import jax.numpy as jnp
import numpy as np
from jax import lax

D = 1024
FF = 4096
VOCAB = 50265
L = 128
CAND_DEV = 1
REF_DEV = 4
SLOTS = 32
CAND_GROUP = 8
REF_GROUP = 64
CANDS = 128
REFS = 512
N_DP = 8
N_PROMPT = 16


def concept_rows(key, picks_tag, noise_tag, sign_tag, shape):
    table = jax.random.normal(jax.random.fold_in(key, 5), (256, D), jnp.float32)
    direction = jax.random.normal(jax.random.fold_in(key, 7), (D,), jnp.float32)
    picks = jax.random.randint(jax.random.fold_in(key, picks_tag), shape[:-1], 0, 256)
    flips = jax.random.bernoulli(jax.random.fold_in(key, sign_tag), 0.5, shape[:2] + (1, 1))
    signs = jnp.where(flips, 1.0, -1.0).astype(jnp.float32)
    shared = 1.5 * signs * direction
    noise_key = jax.random.fold_in(key, noise_tag)
    noise = jax.random.normal(noise_key, shape, jnp.float32)
    values = table[picks] + shared + 0.6 * noise
    return values.astype(jnp.bfloat16)


def draw_cand_hidden(key, part):
    return concept_rows(key, 11, 17, 19, (N_PROMPT * CAND_DEV, N_DP, L, D))


def draw_ref_hidden(key, part):
    return concept_rows(key, 13, 23, 29, (N_DP * REF_DEV, N_PROMPT, L, D))


def draw_pair_count(key, part):
    counts = jax.random.randint(jax.random.fold_in(key, 31), (N_DP * N_PROMPT,), SLOTS // 4, SLOTS + 1)
    chosen = jax.random.randint(jax.random.fold_in(key, 37), (), 0, N_DP * N_PROMPT)
    positions = jnp.arange(N_DP * N_PROMPT, dtype=jnp.int32)
    counts = jnp.where(positions == chosen, SLOTS, counts)
    return counts.reshape(N_DP, N_PROMPT).astype(jnp.int32)


def set_ends(result, stream_key, least, top_value):
    extent = result.shape
    spot = [jax.random.randint(jax.random.fold_in(stream_key, axis), (), 0, extent[axis]) for axis in range(len(extent))]
    result = result.at[tuple(spot)].set(least)
    longest = extent.index(max(extent))
    spot[longest] = (spot[longest] + 1) % extent[longest]
    return result.at[tuple(spot)].set(top_value)


def rank_table(number_of, lean):
    loads = [(1 << 20) // math.isqrt(grade ** lean) + 1 for grade in range(1, number_of + 1)]
    deviation = 1 + sum(loads) // (1 << 30)
    return np.cumsum(np.array([max(1, weight // deviation) for weight in loads]))


def skewed_ids(stream_key, extent, number_of, lean):
    listing = rank_table(number_of, lean)
    ticket = jax.random.randint(jax.random.fold_in(stream_key, 1), extent, 0, int(listing[number_of - 1]))
    rank = jnp.searchsorted(jnp.asarray(listing, jnp.int32), ticket, side="right")
    return jax.random.permutation(jax.random.fold_in(stream_key, 2), number_of)[rank].astype(jnp.int32)


def normal_values(stream_key, extent, scale, bound, kind=jnp.bfloat16):
    drawn = jax.random.normal(stream_key, extent, jnp.float32) * scale
    return jnp.minimum(jnp.maximum(drawn, -bound), bound).astype(kind)


def setup_inputs(seed: int = 0) -> dict:
    key_of = jax.random.split(jax.random.key(seed), 17)
    return {
        "cand_hidden": draw_cand_hidden(jax.random.fold_in(key_of[16], 71), 0),
        "ref_hidden": draw_ref_hidden(jax.random.fold_in(key_of[16], 71), 0),
        "cand_ids": set_ends(skewed_ids(key_of[2], (N_PROMPT * CAND_DEV, N_DP, L), VOCAB, 2), jax.random.fold_in(key_of[2], 3), 0, VOCAB - 1).astype(jnp.int32),
        "ref_ids": set_ends(skewed_ids(key_of[3], (N_DP * REF_DEV, N_PROMPT, L), VOCAB, 2), jax.random.fold_in(key_of[3], 3), 0, VOCAB - 1).astype(jnp.int32),
        "cand_len": set_ends(jax.random.randint(key_of[4], (N_PROMPT * CAND_DEV, N_DP), L // 4, L + 1), jax.random.fold_in(key_of[4], 1), L // 4, L).astype(jnp.int32),
        "reference_length": set_ends(jax.random.randint(key_of[5], (N_DP * REF_DEV, N_PROMPT), L // 4, L + 1), jax.random.fold_in(key_of[5], 1), L // 4, L).astype(jnp.int32),
        "idf_table": jnp.clip(jnp.exp(jax.random.uniform(key_of[6], (VOCAB,), jnp.float32, math.log(1.0), math.log(10.0))), 1.0, 10.0),
        "up_weight": normal_values(key_of[7], (D, FF), D ** -0.5, 0.1875),
        "up_bias": normal_values(key_of[8], (FF,), 0.5, 3.0, jnp.float32),
        "down_weight": normal_values(key_of[9], (FF, D), FF ** -0.5, 0.09375),
        "down_bias": normal_values(key_of[10], (D,), 0.5, 3.0, jnp.float32),
        "norm_gain": jnp.clip(jnp.exp(jax.random.uniform(key_of[11], (D,), jnp.float32, math.log(0.3), math.log(3.0))), 0.3, 3.0),
        "norm_bias": normal_values(key_of[12], (D,), 0.5, 3.0, jnp.float32),
        "pair_cand": set_ends(jax.random.randint(key_of[13], (N_DP, N_PROMPT, SLOTS), 0, CAND_GROUP), jax.random.fold_in(key_of[13], 1), 0, CAND_GROUP - 1).astype(jnp.int32),
        "pair_ref": set_ends(jax.random.randint(key_of[14], (N_DP, N_PROMPT, SLOTS), 0, REF_GROUP), jax.random.fold_in(key_of[14], 1), 0, REF_GROUP - 1).astype(jnp.int32),
        "pair_count": draw_pair_count(jax.random.fold_in(key_of[16], 71), 0),
    }


def encode_rows(hidden, up_weight, up_bias, down_weight, down_bias, norm_gain, norm_bias):
    preactivation_hidden = jnp.dot(hidden, up_weight, preferred_element_type=jnp.float32) + up_bias
    activated = jax.nn.gelu(preactivation_hidden, approximate=False).astype(jnp.bfloat16)
    summed = hidden.astype(jnp.float32) + jnp.dot(activated, down_weight, preferred_element_type=jnp.float32) + down_bias
    center = lax.optimization_barrier(jnp.mean(summed, axis=-1, keepdims=True))
    spread = lax.optimization_barrier(jnp.mean(jnp.square(summed - center), axis=-1, keepdims=True))
    normed = (summed - center) * lax.rsqrt(spread + 1e-05) * norm_gain + norm_bias
    magnitude = lax.optimization_barrier(jnp.sum(jnp.square(normed), axis=-1, keepdims=True))
    return (normed * lax.rsqrt(magnitude + 1e-06)).astype(jnp.bfloat16)

def token_idf_weights(ids, lengths, idf_table):
    positions = jnp.arange(ids.shape[-1], dtype=jnp.int32)
    live_tokens = positions[None, :] < lengths[:, None]
    return jnp.where(live_tokens, idf_table[ids], 0.0).astype(jnp.bfloat16)

def score_pair(candidate_normalized, cand_weight, ref_unit, ref_weight):
    cosine_similarity = jnp.dot(candidate_normalized, ref_unit.T, preferred_element_type=jnp.float32)
    row_best = lax.optimization_barrier(jnp.max(jnp.where(ref_weight[None, :] > 0, cosine_similarity, -10000.0), axis=1))
    col_best = lax.optimization_barrier(jnp.max(jnp.where(cand_weight[:, None] > 0, cosine_similarity, -10000.0), axis=0))
    cand_float = cand_weight.astype(jnp.float32)
    ref_float = ref_weight.astype(jnp.float32)
    precision = jnp.sum(cand_float * row_best) / jnp.sum(cand_float)
    recall = jnp.sum(ref_float * col_best) / jnp.sum(ref_float)
    return (precision, recall)

def reference(cand_hidden, ref_hidden, cand_ids, ref_ids, cand_len, reference_length, idf_table, up_weight, up_bias, down_weight, down_bias, norm_gain, norm_bias, pair_cand, pair_ref, pair_count):

    def encode_one(sequence):
        return encode_rows(sequence, up_weight, up_bias, down_weight, down_bias, norm_gain, norm_bias)
    candidate_normalized = lax.map(encode_one, cand_hidden.reshape(CANDS, L, D))
    ref_unit = lax.map(encode_one, ref_hidden.reshape(REFS, L, D))
    cand_weight = token_idf_weights(cand_ids.reshape(CANDS, L), cand_len.reshape(CANDS), idf_table)
    ref_weight = token_idf_weights(ref_ids.reshape(REFS, L), reference_length.reshape(REFS), idf_table)
    prompt_index = jnp.arange(N_PROMPT, dtype=jnp.int32)[None, :, None]
    shard_index = jnp.arange(N_DP, dtype=jnp.int32)[:, None, None]
    cand_pick = (prompt_index * CAND_GROUP + pair_cand).reshape(-1).astype(jnp.int32)
    ref_pick = (shard_index * REF_GROUP + pair_ref).reshape(-1).astype(jnp.int32)

    def one_pair(indices):
        cand_row, ref_row = indices
        return score_pair(candidate_normalized[cand_row], cand_weight[cand_row], ref_unit[ref_row], ref_weight[ref_row])
    precision, recall = lax.map(one_pair, (cand_pick, ref_pick))
    fmeasure = 2.0 * precision * recall / jnp.maximum(precision + recall, 0.7)
    live_slots = (jnp.arange(SLOTS, dtype=jnp.int32)[None, None, :] < pair_count[:, :, None]).reshape(-1)
    stacked = jnp.where(live_slots[None, :], jnp.stack([precision, recall, fmeasure]), 0.0)
    pair_scores = stacked.reshape(3, N_DP, N_PROMPT, SLOTS)
    totals = lax.optimization_barrier(jnp.sum(stacked, axis=1)) / jnp.sum(live_slots.astype(jnp.float32))
    return (pair_scores, totals)
```

```python
import functools

import jax
import jax.numpy as jnp
from jax import lax
from jax.experimental import pallas as pl
from jax.experimental.pallas import tpu as pltpu
from jax.sharding import PartitionSpec as P

D = 1024
L = 128
SLOTS = 32
TABLE_ROWS = 400
AXES = ("dp", "prompt")
GRID = [(y, c, x, z) for y in range(4) for c in range(2) for x in range(4) for z in range(4)]


def number(y, c, x, z):
    return (((y % 4) * 2 + c) * 4 + x % 4) * 4 + z % 4


def send(value, where):
    return lax.ppermute(value, AXES, [(number(*a), number(*where(*a))) for a in GRID])


def along_x(step):
    return lambda y, c, x, z: (y, c, x + (step if c == 0 else -step), z)


def along_first(step):
    return lambda y, c, x, z: (y + step, c, x, z) if c == 0 else (y, c, x, z + step)


def along_second(step):
    return lambda y, c, x, z: (y, c, x, z + step) if c == 0 else (y + step, c, x, z)


def along_z(step):
    return lambda y, c, x, z: (y, c, x, z + step)


def to_other_core(y, c, x, z):
    return (y, 1 - c, x, z)


def encode_kernel(
    sub, clen_ref, rlen_ref, cid_ref, rid_ref, tbl_ref, ch_ref, rh_ref, up, upb, dn, dnb, gain, bias,
    co_ref, ro_ref, x_ref, acc_ref,
):
    step = pl.program_id(0)

    def token_weights(ids, length):
        high, low = ids >> 7, ids & 127
        hot = (lax.broadcasted_iota(jnp.int32, (TABLE_ROWS, L), 0) == high).astype(jnp.bfloat16)
        rows = lax.dot_general(
            tbl_ref[...], hot, (((0,), (0,)), ((), ())), preferred_element_type=jnp.float32
        )
        mine = lax.broadcasted_iota(jnp.int32, (128, L), 0) == low
        value = jnp.sum(jnp.where(mine, rows, 0.0), axis=0, keepdims=True)
        live = lax.broadcasted_iota(jnp.int32, (1, L), 1) < length
        return jnp.where(live, value, 0.0)

    @pl.when(step == 0)
    def _():
        x_ref[0:L, :] = ch_ref[0]
        for q in range(4):
            x_ref[L * (q + 1) : L * (q + 2), :] = rh_ref[q]
        row = lax.broadcasted_iota(jnp.int32, (16, L), 0)
        co_ref[L:, :] = jnp.zeros((16, D), jnp.bfloat16)
        ro_ref[4 * L :, :] = jnp.zeros((16, D), jnp.bfloat16)
        w = token_weights(cid_ref[...], clen_ref[0])
        co_ref[L:, 0:L] = jnp.where(row == 0, w, 0.0).astype(jnp.bfloat16)
        block = jnp.zeros((16, L), jnp.float32)
        for q in range(4):
            block = jnp.where(row == q, token_weights(rid_ref[q : q + 1, :], rlen_ref[q]), block)
        ro_ref[4 * L :, 0:L] = block.astype(jnp.bfloat16)

    w = up.shape[1] // sub
    x = x_ref[...]
    pre = [
        jnp.dot(x, up[:, k * w : (k + 1) * w], preferred_element_type=jnp.float32)
        + upb[:, k * w : (k + 1) * w]
        for k in range(sub)
    ]
    part = None
    for k in range(sub):
        h = pre[k]
        act = (0.5 * h * (lax.erf(h * 0.7071067811865476) + 1.0)).astype(jnp.bfloat16)
        d = jnp.dot(act, dn[k * w : (k + 1) * w, :], preferred_element_type=jnp.float32)
        part = d if part is None else part + d

    @pl.when(step == 0)
    def _():
        acc_ref[...] = part

    @pl.when(step > 0)
    def _():
        acc_ref[...] += part

    @pl.when(step == pl.num_programs(0) - 1)
    def _():
        for c in range(0, 5 * L, 64):
            r = slice(c, c + 64)
            s = x_ref[r, :].astype(jnp.float32) + acc_ref[r, :] + dnb[...]
            center = jnp.mean(s, axis=-1, keepdims=True)
            e = s - center
            spread = jnp.mean(e * e, axis=-1, keepdims=True)
            y = e * lax.rsqrt(spread + 1e-5) * gain[...] + bias[...]
            m = jnp.sum(y * y, axis=-1, keepdims=True)
            unit = (y * lax.rsqrt(m + 1e-6)).astype(jnp.bfloat16)
            if c < L:
                co_ref[r, :] = unit
            else:
                ro_ref[c - L : c - L + 64, :] = unit


def encode(ch, rh, cids, rids, clen, rlen, table, up, upb, dn, dnb, gain, bias, f=1024, sub=4):
    def full(a):
        return pl.BlockSpec(a.shape, lambda i: (0,) * a.ndim, pipeline_mode=pl.Buffered(1))

    smem = pl.BlockSpec(memory_space=pltpu.SMEM)
    outs = [
        jax.ShapeDtypeStruct((L + 16, D), jnp.bfloat16),
        jax.ShapeDtypeStruct((4 * L + 16, D), jnp.bfloat16),
    ]
    return pl.pallas_call(
        functools.partial(encode_kernel, sub),
        grid=(up.shape[1] // f,),
        in_specs=[smem, smem, full(cids), full(rids), full(table), full(ch), full(rh)]
        + [
            pl.BlockSpec((D, f), lambda i: (0, i)),
            pl.BlockSpec((1, f), lambda i: (0, i)),
            pl.BlockSpec((f, D), lambda i: (i, 0)),
            full(dnb),
            full(gain),
            full(bias),
        ],
        out_specs=[pl.BlockSpec(o.shape, lambda i: (0, 0)) for o in outs],
        out_shape=outs,
        scratch_shapes=[pltpu.VMEM((5 * L, D), jnp.bfloat16), pltpu.VMEM((5 * L, D), jnp.float32)],
        compiler_params=pltpu.CompilerParams(
            dimension_semantics=("arbitrary",), vmem_limit_bytes=60 << 20
        ),
        name="encode",
    )(clen, rlen, cids, rids, table, ch, rh, up, upb, dn, dnb, gain, bias)


SLOT_BUFS = 4


def pair_kernel(
    pos_ref, l0, l1, l2, l3,
    own4, d1, d2, d3, d4, e0, e1, e2, e3, e4, r0, ra1, ra2, rb,
    out_ref, cbuf, rbuf, wbuf, todo, sem_c, sem_r, sem_w,
):
    y, core, x, z = pos_ref[0], pos_ref[1], pos_ref[2], pos_ref[3]
    n = jnp.int32(0)
    for lst, dz in ((l0, 0), (l1, 3), (l2, 1), (l3, 2)):
        zj = (z + dz) & 3

        def scan(s, n, lst=lst, dz=dz, zj=zj):
            c = lst[0, s]
            r = lst[0, SLOTS + s]
            mine = (r & 3) == z

            @pl.when(mine)
            def _():
                kc = c & 1
                dy = ((c >> 1) - y) & 3
                u1 = jnp.where(kc == 0, dy, dz)
                u2 = jnp.where(kc == 0, dz, dy)
                i1 = (u1 == 3) * 1 + (u1 == 1) * 2 + (u1 == 2) * 3
                g2 = (u2 == 3) * 1 + (u2 == 1) * 2 + (u2 == 2) * 3
                g2 = jnp.where((g2 == 3) & (i1 >= 2), 4, g2)
                src = g2 + jnp.where(kc == core, 0, 5)
                row = jnp.where(g2 == 4, i1 - 2, i1)
                dx = (((r & 15) >> 2) - x) & 3
                back = jnp.where(core == 0, 3, 1)
                rs = jnp.where(dx == 0, 0, jnp.where(dx == 2, 3, jnp.where(dx == back, 1, 2)))
                todo[0, n] = src
                todo[1, n] = row
                todo[2, n] = rs
                todo[3, n] = r >> 4
                todo[4, n] = zj * SLOTS + s

            return n + jnp.where(mine, 1, 0)

        n = lax.fori_loop(0, lst[0, 2 * SLOTS], scan, n)

    def start(t, b):
        row, i = todo[1, t], todo[3, t]
        for k, buf in enumerate((own4, d1, d2, d3, d4, e0, e1, e2, e3, e4)):
            @pl.when(todo[0, t] == k)
            def _():
                pltpu.make_async_copy(buf.at[row], cbuf.at[b], sem_c.at[b]).start()
        at = pl.multiple_of(i * L, L)
        for k, buf in enumerate((r0, ra1, ra2, rb)):
            @pl.when(todo[2, t] == k)
            def _():
                pltpu.make_async_copy(buf.at[pl.ds(at, L), :], rbuf.at[b], sem_r.at[b]).start()
                pltpu.make_async_copy(
                    buf.at[pl.ds(4 * L, 16), pl.ds(0, L)], wbuf.at[b], sem_w.at[b]
                ).start()

    for t in range(SLOT_BUFS - 1):
        @pl.when(t < n)
        def _(t=t):
            start(t, t)

    lane = lax.broadcasted_iota(jnp.int32, (8, L), 1)
    sub = lax.broadcasted_iota(jnp.int32, (8, L), 0)
    eye = lax.broadcasted_iota(jnp.int32, (L, L), 0) == lax.broadcasted_iota(jnp.int32, (L, L), 1)

    def score(t, carry):
        acc, total = carry
        b = t % SLOT_BUFS

        @pl.when(t + SLOT_BUFS - 1 < n)
        def _():
            start(t + SLOT_BUFS - 1, (t + SLOT_BUFS - 1) % SLOT_BUFS)

        pltpu.make_async_copy(own4.at[0], cbuf.at[b], sem_c.at[b]).wait()
        pltpu.make_async_copy(r0.at[pl.ds(0, L), :], rbuf.at[b], sem_r.at[b]).wait()
        pltpu.make_async_copy(r0.at[pl.ds(4 * L, 16), pl.ds(0, L)], wbuf.at[b], sem_w.at[b]).wait()
        similar = lax.dot_general(
            cbuf[b, 0:L, :], rbuf[b], (((1,), (1,)), ((), ())), preferred_element_type=jnp.float32
        )
        cw = cbuf[b, L:, 0:L].astype(jnp.float32)[0:1, :]
        wide = wbuf[b].astype(jnp.float32)
        rsub = lax.broadcasted_iota(jnp.int32, (16, L), 0)
        rw = jnp.sum(jnp.where(rsub == todo[3, t], wide, 0.0), axis=0, keepdims=True)
        cw_col = jnp.sum(jnp.where(eye, cw, 0.0), axis=1, keepdims=True)
        row_best = jnp.max(jnp.where(rw > 0, similar, -10000.0), axis=1, keepdims=True)
        col_best = jnp.max(jnp.where(cw_col > 0, similar, -10000.0), axis=0, keepdims=True)
        precision = jnp.sum(cw_col * row_best, axis=0, keepdims=True) / jnp.sum(
            cw, axis=1, keepdims=True
        )
        recall = jnp.sum(rw * col_best, axis=1, keepdims=True) / jnp.sum(rw, axis=1, keepdims=True)
        fmeasure = 2.0 * precision * recall / jnp.maximum(precision + recall, 0.7)
        three = jnp.where(
            sub == 0, precision, jnp.where(sub == 1, recall, jnp.where(sub == 2, fmeasure, 0.0))
        )
        return jnp.where(lane == todo[4, t], three, acc), total + three

    zero = jnp.zeros((8, L), jnp.float32)
    acc, total = lax.fori_loop(0, n, score, (zero, zero))
    count = l0[0, 2 * SLOTS].astype(jnp.float32)
    sums = jnp.where(
        lane == 0, total[0:1, :], jnp.where(lane == 1, total[1:2, :], jnp.where(lane == 2, total[2:3, :], count))
    )
    sums = jnp.where((sub == 3) & (lane < 4), sums, 0.0)
    for q in range(out_ref.shape[0]):
        out_ref[q] = sums
    mine = (y * 2 + core) * 4 + x
    for q in range(4):
        out_ref[mine * 4 + q] = jnp.where(sub < 3, acc, sums)


def score_pairs(pos, lists, bufs):
    smem = pl.BlockSpec(memory_space=pltpu.SMEM)
    hbm = pl.BlockSpec(memory_space=pl.ANY)
    return pl.pallas_call(
        pair_kernel,
        in_specs=[smem] * 5 + [hbm] * len(bufs),
        out_specs=pl.BlockSpec(memory_space=pltpu.VMEM),
        out_shape=jax.ShapeDtypeStruct((128, 8, L), jnp.float32),
        scratch_shapes=[
            pltpu.VMEM((SLOT_BUFS, L + 16, D), jnp.bfloat16),
            pltpu.VMEM((SLOT_BUFS, L, D), jnp.bfloat16),
            pltpu.VMEM((SLOT_BUFS, 16, L), jnp.bfloat16),
            pltpu.SMEM((5, 4 * SLOTS), jnp.int32),
            pltpu.SemaphoreType.DMA((SLOT_BUFS,)),
            pltpu.SemaphoreType.DMA((SLOT_BUFS,)),
            pltpu.SemaphoreType.DMA((SLOT_BUFS,)),
        ],
        compiler_params=pltpu.CompilerParams(vmem_limit_bytes=60 << 20),
        name="score_pairs",
    )(pos, *lists, *bufs)


def on_device(
    cand_hidden, ref_hidden, cand_ids, ref_ids, cand_len, reference_length, idf_table, up_weight,
    up_bias, down_weight, down_bias, norm_gain, norm_bias, pair_cand, pair_ref, pair_count,
):
    table = jnp.pad(idf_table, (0, TABLE_ROWS * 128 - idf_table.shape[0]))
    table = table.reshape(TABLE_ROWS, 128).astype(jnp.bfloat16)
    cand, refs = encode(
        cand_hidden.reshape(1, L, D),
        ref_hidden.reshape(4, L, D),
        cand_ids.reshape(1, L),
        ref_ids.reshape(4, L),
        cand_len.reshape(1),
        reference_length.reshape(4),
        table,
        up_weight,
        up_bias.reshape(1, -1),
        down_weight,
        down_bias.reshape(1, -1),
        norm_gain.reshape(1, -1),
        norm_bias.reshape(1, -1),
    )
    ref_back = send(refs, along_x(1))
    ref_ahead = send(refs, along_x(-1))
    c1 = send(cand, along_first(1))
    c2 = send(cand, along_first(-1))
    c3 = send(c1, along_first(1))
    own4 = jnp.stack([cand, c1, c2, c3])
    d1 = send(own4, along_second(1))
    d2 = send(own4, along_second(-1))
    d3 = send(d1[:2], along_second(1))
    d4 = send(d2[2:], along_second(-1))
    others = [send(v, to_other_core) for v in (own4, d1, d2, d3, d4)]
    ref_far = send(ref_back, along_x(1))
    slots = jnp.concatenate(
        [
            pair_cand.reshape(-1),
            pair_ref.reshape(-1),
            jnp.broadcast_to(pair_count.reshape(1), (2 * SLOTS,)),
        ]
    ).reshape(1, 4 * SLOTS)
    lists = [slots] + [send(slots, along_z(k)) for k in (1, -1, 2)]
    dp, prompt = lax.axis_index("dp"), lax.axis_index("prompt")
    z = prompt & 3
    pos = jnp.stack([dp >> 1, dp & 1, prompt >> 2, z]).astype(jnp.int32)
    payload = score_pairs(
        pos, lists, [own4, d1, d2, d3, d4, *others, refs, ref_back, ref_ahead, ref_far]
    )
    got = jnp.sum(lax.all_to_all(payload, AXES, 0, 0), axis=0)
    scores = lax.dynamic_slice(got, (0, z * SLOTS), (3, SLOTS))
    return scores.reshape(3, 1, 1, SLOTS), got[3, :3] / got[3, 3]


def solution(mesh):
    placed = (
        P("prompt", "dp", None, None),
        P("dp", "prompt", None, None),
        P("prompt", "dp", None),
        P("dp", "prompt", None),
        P("prompt", "dp"),
        P("dp", "prompt"),
        P(),
        P(),
        P(),
        P(),
        P(),
        P(),
        P(),
        P("dp", "prompt", None),
        P("dp", "prompt", None),
        P("dp", "prompt"),
    )
    return jax.shard_map(
        on_device,
        mesh=mesh,
        in_specs=placed,
        out_specs=(P(None, "dp", "prompt", None), P()),
        check_vma=False,
    )
```

```python
import functools

import jax
import jax.numpy as jnp
from jax import lax
from jax.experimental import pallas as pl
from jax.experimental.pallas import tpu as pltpu
from jax.sharding import PartitionSpec as P

D = 1024
L = 128
SLOTS = 32
TABLE_ROWS = 400
AXES = ("dp", "prompt")
GRID = [(y, c, x, z) for y in range(4) for c in range(2) for x in range(4) for z in range(4)]


def number(y, c, x, z):
    return (((y % 4) * 2 + c) * 4 + x % 4) * 4 + z % 4


def send(value, where):
    return lax.ppermute(value, AXES, [(number(*a), number(*where(*a))) for a in GRID])


def along_x(step):
    return lambda y, c, x, z: (y, c, x + (step if c == 0 else -step), z)


def along_first(step):
    return lambda y, c, x, z: (y + step, c, x, z) if c == 0 else (y, c, x, z + step)


def along_second(step):
    return lambda y, c, x, z: (y, c, x, z + step) if c == 0 else (y + step, c, x, z)


def along_z(step):
    return lambda y, c, x, z: (y, c, x, z + step)


def to_other_core(y, c, x, z):
    return (y, 1 - c, x, z)


def encode_kernel(n_cand, picks, weights, sub, *refs):
    refs = list(refs)
    if weights:
        clen_ref, rlen_ref, cid_ref, rid_ref, tbl_ref = refs[:5]
        refs = refs[5:]
    ch_ref = refs.pop(0) if n_cand else None
    rh_ref, up, upb, dn, dnb, gain, bias = refs[:7]
    refs = refs[7:]
    co_ref = refs.pop(0) if n_cand else None
    ro_ref, x_ref, acc_ref = refs
    step = pl.program_id(0)
    seqs = n_cand + len(picks)

    def token_weights(ids, length):
        high, low = ids >> 7, ids & 127
        hot = (lax.broadcasted_iota(jnp.int32, (TABLE_ROWS, L), 0) == high).astype(jnp.bfloat16)
        rows = lax.dot_general(
            tbl_ref[...], hot, (((0,), (0,)), ((), ())), preferred_element_type=jnp.float32
        )
        mine = lax.broadcasted_iota(jnp.int32, (128, L), 0) == low
        value = jnp.sum(jnp.where(mine, rows, 0.0), axis=0, keepdims=True)
        live = lax.broadcasted_iota(jnp.int32, (1, L), 1) < length
        return jnp.where(live, value, 0.0)

    @pl.when(step == 0)
    def _():
        if n_cand:
            x_ref[0:L, :] = ch_ref[0]
        for k, q in enumerate(picks):
            x_ref[L * (n_cand + k) : L * (n_cand + k + 1), :] = rh_ref[q]
        if weights:
            row = lax.broadcasted_iota(jnp.int32, (16, L), 0)
            co_ref[L:, :] = jnp.zeros((16, D), jnp.bfloat16)
            ro_ref[len(picks) * L :, :] = jnp.zeros((16, D), jnp.bfloat16)
            w = token_weights(cid_ref[...], clen_ref[0])
            co_ref[L:, 0:L] = jnp.where(row == 0, w, 0.0).astype(jnp.bfloat16)
            block = jnp.zeros((16, L), jnp.float32)
            for q in range(4):
                block = jnp.where(row == q, token_weights(rid_ref[q : q + 1, :], rlen_ref[q]), block)
            ro_ref[len(picks) * L :, 0:L] = block.astype(jnp.bfloat16)

    w = up.shape[1] // sub
    x = x_ref[...]
    pre = [
        jnp.dot(x, up[:, k * w : (k + 1) * w], preferred_element_type=jnp.float32)
        + upb[:, k * w : (k + 1) * w]
        for k in range(sub)
    ]
    part = None
    for k in range(sub):
        h = pre[k]
        act = (0.5 * h * (lax.erf(h * 0.7071067811865476) + 1.0)).astype(jnp.bfloat16)
        d = jnp.dot(act, dn[k * w : (k + 1) * w, :], preferred_element_type=jnp.float32)
        part = d if part is None else part + d

    @pl.when(step == 0)
    def _():
        acc_ref[...] = part

    @pl.when(step > 0)
    def _():
        acc_ref[...] += part

    @pl.when(step == pl.num_programs(0) - 1)
    def _():
        for c in range(0, seqs * L, 64):
            r = slice(c, c + 64)
            s = x_ref[r, :].astype(jnp.float32) + acc_ref[r, :] + dnb[...]
            center = jnp.mean(s, axis=-1, keepdims=True)
            e = s - center
            spread = jnp.mean(e * e, axis=-1, keepdims=True)
            y = e * lax.rsqrt(spread + 1e-5) * gain[...] + bias[...]
            m = jnp.sum(y * y, axis=-1, keepdims=True)
            unit = (y * lax.rsqrt(m + 1e-6)).astype(jnp.bfloat16)
            if c < L * n_cand:
                co_ref[r, :] = unit
            else:
                ro_ref[c - L * n_cand : c - L * n_cand + 64, :] = unit


def encode(picks, cand, rh, words, layer, f=1024, sub=4):
    def full(a):
        return pl.BlockSpec(a.shape, lambda i: (0,) * a.ndim, pipeline_mode=pl.Buffered(1))

    up, upb, dn, dnb, gain, bias = layer
    n_cand = 0 if cand is None else 1
    extra = 16 if words else 0
    seqs = n_cand + len(picks)
    smem = pl.BlockSpec(memory_space=pltpu.SMEM)
    outs = [jax.ShapeDtypeStruct((L + extra, D), jnp.bfloat16)] * n_cand + [
        jax.ShapeDtypeStruct((len(picks) * L + extra, D), jnp.bfloat16)
    ]
    first = list(words) + ([cand] if n_cand else []) + [rh]
    return pl.pallas_call(
        functools.partial(encode_kernel, n_cand, picks, bool(words), sub),
        grid=(up.shape[1] // f,),
        in_specs=[smem if k < 2 and words else full(a) for k, a in enumerate(first)]
        + [
            pl.BlockSpec((D, f), lambda i: (0, i)),
            pl.BlockSpec((1, f), lambda i: (0, i)),
            pl.BlockSpec((f, D), lambda i: (i, 0)),
            full(dnb),
            full(gain),
            full(bias),
        ],
        out_specs=[pl.BlockSpec(o.shape, lambda i: (0, 0)) for o in outs],
        out_shape=outs,
        scratch_shapes=[
            pltpu.VMEM((seqs * L, D), jnp.bfloat16),
            pltpu.VMEM((seqs * L, D), jnp.float32),
        ],
        compiler_params=pltpu.CompilerParams(
            dimension_semantics=("arbitrary",), vmem_limit_bytes=60 << 20
        ),
        cost_estimate=pl.CostEstimate(
            flops=4 * seqs * L * D * up.shape[1], bytes_accessed=17 << 20, transcendentals=0
        ),
        name="encode",
    )(*first, up, upb, dn, dnb, gain, bias)


GROUP = 4


def score_listed(todo, n, acc, total, cands, refs, cbuf, rbuf, wbuf, sem):
    def start(t, b):
        for k, buf in enumerate(cands):
            @pl.when(todo[0, t] == k)
            def _():
                pltpu.make_async_copy(buf.at[todo[1, t]], cbuf.at[b], sem.at[0, b]).start()
        at = pl.multiple_of(todo[3, t] * L, L)
        for k, buf in enumerate(refs):
            @pl.when(todo[2, t] == k)
            def _():
                words = refs[k - k % 2]
                pltpu.make_async_copy(buf.at[pl.ds(at, L), :], rbuf.at[b], sem.at[1, b]).start()
                pltpu.make_async_copy(
                    words.at[pl.ds(2 * L, 16), pl.ds(0, L)], wbuf.at[b], sem.at[2, b]
                ).start()

    def start_group(g):
        for k in range(GROUP):
            t = g * GROUP + k

            @pl.when(t < n)
            def _(t=t, k=k):
                start(t, (g % 2) * GROUP + k)

    start_group(0)
    lane = lax.broadcasted_iota(jnp.int32, (8, L), 1)
    sub = lax.broadcasted_iota(jnp.int32, (8, L), 0)
    eye = lax.broadcasted_iota(jnp.int32, (L, L), 0) == lax.broadcasted_iota(jnp.int32, (L, L), 1)

    def one(t, b):
        similar = lax.dot_general(
            cbuf[b, 0:L, :], rbuf[b], (((1,), (1,)), ((), ())), preferred_element_type=jnp.float32
        )
        cw = cbuf[b, L:, 0:L].astype(jnp.float32)[0:1, :]
        wide = wbuf[b].astype(jnp.float32)
        rsub = lax.broadcasted_iota(jnp.int32, (16, L), 0)
        rw = jnp.sum(jnp.where(rsub == todo[4, t], wide, 0.0), axis=0, keepdims=True)
        cw_col = jnp.sum(jnp.where(eye, cw, 0.0), axis=1, keepdims=True)
        row_best = jnp.max(jnp.where(rw > 0, similar, -10000.0), axis=1, keepdims=True)
        col_best = jnp.max(jnp.where(cw_col > 0, similar, -10000.0), axis=0, keepdims=True)
        precision = jnp.sum(cw_col * row_best, axis=0, keepdims=True) / jnp.sum(
            cw, axis=1, keepdims=True
        )
        recall = jnp.sum(rw * col_best, axis=1, keepdims=True) / jnp.sum(rw, axis=1, keepdims=True)
        fmeasure = 2.0 * precision * recall / jnp.maximum(precision + recall, 0.7)
        return precision, recall, fmeasure

    def group(g, carry):
        acc, total = carry
        start_group(g + 1)
        for k in range(GROUP):
            b = (g % 2) * GROUP + k

            @pl.when(g * GROUP + k < n)
            def _(b=b):
                pltpu.make_async_copy(cands[0].at[0], cbuf.at[b], sem.at[0, b]).wait()
                pltpu.make_async_copy(refs[0].at[pl.ds(0, L), :], rbuf.at[b], sem.at[1, b]).wait()
                pltpu.make_async_copy(
                    refs[0].at[pl.ds(2 * L, 16), pl.ds(0, L)], wbuf.at[b], sem.at[2, b]
                ).wait()

        scores = []
        for k in range(GROUP):
            t = jnp.minimum(g * GROUP + k, n - 1)
            scores.append((t, g * GROUP + k < n, one(t, (g % 2) * GROUP + k)))
        for t, real, (p, r, f) in scores:
            three = jnp.where(lane < 32, p, jnp.where(lane < 64, r, f))
            here = (sub == todo[5, t]) & ((lane & 31) == todo[6, t]) & (lane < 96) & real
            acc = jnp.where(here, three, acc)
            rows = jnp.where(sub == 0, p, jnp.where(sub == 1, r, f))
            total = total + jnp.where(real, rows, 0.0)
        return acc, total

    return lax.fori_loop(0, (n + GROUP - 1) // GROUP, group, (acc, total))


def early_kernel(pos_ref, l0, l1, l2, l3, *refs):
    cands, refs_, (out_ref, later, cbuf, rbuf, wbuf, todo, sem) = refs[:10], refs[10:16], refs[16:]
    y, core, x, z = pos_ref[0], pos_ref[1], pos_ref[2], pos_ref[3]
    n = m = jnp.int32(0)
    for lst, dz in ((l0, 0), (l1, 3), (l2, 1), (l3, 2)):
        zj = (z + dz) & 3

        def scan(s, counts, lst=lst, dz=dz, zj=zj):
            n, m = counts
            c = lst[0, s]
            r = lst[0, SLOTS + s]
            mine = (r & 3) == z
            dx = (((r & 15) >> 2) - x) & 3
            late = mine & (dx == 2)
            soon = mine & (dx != 2)
            kc = c & 1
            dy = ((c >> 1) - y) & 3
            u1 = jnp.where(kc == 0, dy, dz)
            u2 = jnp.where(kc == 0, dz, dy)
            i1 = (4 - u1) & 3
            g2 = (u2 == 3) * 1 + (u2 == 1) * 2 + (u2 == 2) * 3
            g2 = jnp.where((g2 == 3) & (i1 >= 2), 4, g2)
            src = g2 + jnp.where(kc == core, 0, 5)
            row = jnp.where(g2 == 4, i1 - 2, i1)
            i = r >> 4
            back = jnp.where(core == 0, 3, 1)
            rs = jnp.where(dx == 0, 0, jnp.where(dx == 2, 3, jnp.where(dx == back, 1, 2)))

            def put(where, k, rs):
                where[0, k] = src
                where[1, k] = row
                where[2, k] = rs * 2 + (i >> 1)
                where[3, k] = i & 1
                where[4, k] = i
                where[5, k] = zj
                where[6, k] = s

            @pl.when(soon)
            def _():
                put(todo, n, rs)

            @pl.when(late)
            def _():
                put(later, m, 0)

            return n + jnp.where(soon, 1, 0), m + jnp.where(late, 1, 0)

        n, m = lax.fori_loop(0, lst[0, 2 * SLOTS], scan, (n, m))
    later[7, 0] = m
    zero = jnp.zeros((8, L), jnp.float32)
    acc, total = score_listed(todo, n, zero, zero, cands, refs_, cbuf, rbuf, wbuf, sem)
    out_ref[0] = acc
    out_ref[1] = total


def late_kernel(pos_ref, l0, todo, *refs):
    cands, refs_, (part, out_ref, cbuf, rbuf, wbuf, sem) = refs[:10], refs[10:12], refs[12:]
    y, core, x = pos_ref[0], pos_ref[1], pos_ref[2]
    acc, total = score_listed(todo, todo[7, 0], part[0], part[1], cands, refs_, cbuf, rbuf, wbuf, sem)
    lane = lax.broadcasted_iota(jnp.int32, (1, L), 1)
    count = l0[0, 2 * SLOTS].astype(jnp.float32)
    sums = jnp.where(
        lane == 96,
        total[0:1, :],
        jnp.where(lane == 97, total[1:2, :], jnp.where(lane == 98, total[2:3, :], count)),
    )
    sums = jnp.where((lane >= 96) & (lane < 100), sums, 0.0)
    for q in range(out_ref.shape[0]):
        out_ref[q] = sums
    mine = (y * 2 + core) * 4 + x
    for q in range(4):
        out_ref[mine * 4 + q] = acc[q : q + 1, :] + sums


def pair_call(kernel, name, smem_args, hbm_args, vmem_args, out_specs, out_shape, scratch):
    smem = pl.BlockSpec(memory_space=pltpu.SMEM)
    hbm = pl.BlockSpec(memory_space=pl.ANY)
    vmem = pl.BlockSpec(memory_space=pltpu.VMEM)
    return pl.pallas_call(
        kernel,
        in_specs=[smem] * len(smem_args) + [hbm] * len(hbm_args) + [vmem] * len(vmem_args),
        out_specs=out_specs,
        out_shape=out_shape,
        scratch_shapes=[
            pltpu.VMEM((2 * GROUP, L + 16, D), jnp.bfloat16),
            pltpu.VMEM((2 * GROUP, L, D), jnp.bfloat16),
            pltpu.VMEM((2 * GROUP, 16, L), jnp.bfloat16),
            *scratch,
            pltpu.SemaphoreType.DMA((3, 2 * GROUP)),
        ],
        compiler_params=pltpu.CompilerParams(vmem_limit_bytes=60 << 20),
        cost_estimate=pl.CostEstimate(
            flops=1 << 30, bytes_accessed=16 << 20, transcendentals=0
        ),
        name=name,
    )(*smem_args, *hbm_args, *vmem_args)


def on_device(
    cand_hidden, ref_hidden, cand_ids, ref_ids, cand_len, reference_length, idf_table, up_weight,
    up_bias, down_weight, down_bias, norm_gain, norm_bias, pair_cand, pair_ref, pair_count,
):
    table = jnp.pad(idf_table, (0, TABLE_ROWS * 128 - idf_table.shape[0]))
    table = table.reshape(TABLE_ROWS, 128).astype(jnp.bfloat16)
    layer = (
        up_weight,
        up_bias.reshape(1, -1),
        down_weight,
        down_bias.reshape(1, -1),
        norm_gain.reshape(1, -1),
        norm_bias.reshape(1, -1),
    )
    hidden = ref_hidden.reshape(4, L, D)
    words = (
        cand_len.reshape(1),
        reference_length.reshape(4),
        cand_ids.reshape(1, L),
        ref_ids.reshape(4, L),
        table,
    )
    cand, refs_a = encode((0, 1), cand_hidden.reshape(1, L, D), hidden, words, layer)
    back_a = send(refs_a, along_x(1))
    ahead_a = send(refs_a, along_x(-1))
    c1 = send(cand, along_first(1))
    c3 = send(cand, along_first(-1))
    c2 = send(cand, along_first(2))
    (refs_b,) = encode((2, 3), None, hidden, (), layer)
    back_a, ahead_a, c1, c2, c3, refs_b = lax.optimization_barrier(
        (back_a, ahead_a, c1, c2, c3, refs_b)
    )
    back_b = send(refs_b, along_x(1))
    ahead_b = send(refs_b, along_x(-1))
    far_a = send(back_a, along_x(1))
    own4 = jnp.stack([cand, c1, c2, c3])
    d1 = send(own4, along_second(1))
    d2 = send(own4, along_second(-1))
    d3 = send(d1[:2], along_second(1))
    d4 = send(d2[2:], along_second(-1))
    d3, d4, far_a, back_b, ahead_b = lax.optimization_barrier((d3, d4, far_a, back_b, ahead_b))
    far_b = send(back_b, along_x(1))
    others = [send(v, to_other_core) for v in (own4, d1, d2, d3, d4)]
    cands = [own4, d1, d2, d3, d4, *others]
    slots = jnp.concatenate(
        [
            pair_cand.reshape(-1),
            pair_ref.reshape(-1),
            jnp.broadcast_to(pair_count.reshape(1), (2 * SLOTS,)),
        ]
    ).reshape(1, 4 * SLOTS)
    lists = [slots] + [send(slots, along_z(k)) for k in (1, -1, 2)]
    dp, prompt = lax.axis_index("dp"), lax.axis_index("prompt")
    pos = jnp.stack([dp >> 1, dp & 1, prompt >> 2, prompt & 3]).astype(jnp.int32)
    part, later = pair_call(
        early_kernel,
        "score_early",
        [pos, *lists],
        [*cands, refs_a, refs_b, back_a, back_b, ahead_a, ahead_b],
        [],
        [pl.BlockSpec(memory_space=pltpu.VMEM), pl.BlockSpec(memory_space=pltpu.SMEM)],
        [
            jax.ShapeDtypeStruct((2, 8, L), jnp.float32),
            jax.ShapeDtypeStruct((8, 4 * SLOTS), jnp.int32),
        ],
        [pltpu.SMEM((8, 4 * SLOTS), jnp.int32)],
    )
    payload = pair_call(
        late_kernel,
        "score_late",
        [pos, slots, later],
        [*cands, far_a, far_b],
        [part],
        pl.BlockSpec(memory_space=pltpu.VMEM),
        jax.ShapeDtypeStruct((128, 1, L), jnp.float32),
        [],
    )
    got = jnp.sum(lax.all_to_all(payload, AXES, 0, 0), axis=0)
    scores = got[:, : 3 * SLOTS].reshape(3, 1, 1, SLOTS)
    return scores, got[0, 96:99] / got[0, 99]


def solution(mesh):
    placed = (
        P("prompt", "dp", None, None),
        P("dp", "prompt", None, None),
        P("prompt", "dp", None),
        P("dp", "prompt", None),
        P("prompt", "dp"),
        P("dp", "prompt"),
        P(),
        P(),
        P(),
        P(),
        P(),
        P(),
        P(),
        P("dp", "prompt", None),
        P("dp", "prompt", None),
        P("dp", "prompt"),
    )
    return jax.shard_map(
        on_device,
        mesh=mesh,
        in_specs=placed,
        out_specs=(P(None, "dp", "prompt", None), P()),
        check_vma=False,
    )
```

```python
import functools

import jax
import jax.numpy as jnp
from jax import lax
from jax.experimental import pallas as pl
from jax.experimental.pallas import tpu as pltpu
from jax.sharding import PartitionSpec as P

D = 1024
L = 128
SLOTS = 32
TABLE_ROWS = 400
AXES = ("dp", "prompt")
GRID = [(y, c, x, z) for y in range(4) for c in range(2) for x in range(4) for z in range(4)]


def number(y, c, x, z):
    return (((y % 4) * 2 + c) * 4 + x % 4) * 4 + z % 4


def send(value, where):
    return lax.ppermute(value, AXES, [(number(*a), number(*where(*a))) for a in GRID])


def along_x(step):
    return lambda y, c, x, z: (y, c, x + (step if c == 0 else -step), z)


def along_first(step):
    return lambda y, c, x, z: (y + step, c, x, z) if c == 0 else (y, c, x, z + step)


def along_second(step):
    return lambda y, c, x, z: (y, c, x, z + step) if c == 0 else (y + step, c, x, z)


def along_z(step):
    return lambda y, c, x, z: (y, c, x, z + step)


def to_other_core(y, c, x, z):
    return (y, 1 - c, x, z)


def encode_kernel(n_cand, picks, weights, sub, *refs):
    refs = list(refs)
    if weights:
        clen_ref, rlen_ref, count_ref, cid_ref, rid_ref, pc_ref, pr_ref, tbl_ref = refs[:8]
        refs = refs[8:]
    ch_ref = refs.pop(0) if n_cand else None
    rh_ref, up, upb, dn, dnb, gain, bias = refs[:7]
    refs = refs[7:]
    co_ref = refs.pop(0) if n_cand else None
    ro_ref, x_ref, acc_ref = refs
    step = pl.program_id(0)
    seqs = n_cand + len(picks)

    def token_weights(ids, length):
        high, low = ids >> 7, ids & 127
        hot = (lax.broadcasted_iota(jnp.int32, (TABLE_ROWS, L), 0) == high).astype(jnp.bfloat16)
        rows = lax.dot_general(
            tbl_ref[...].astype(jnp.bfloat16), hot, (((0,), (0,)), ((), ())), preferred_element_type=jnp.float32
        )
        mine = lax.broadcasted_iota(jnp.int32, (128, L), 0) == low
        value = jnp.sum(jnp.where(mine, rows, 0.0), axis=0, keepdims=True)
        live = lax.broadcasted_iota(jnp.int32, (1, L), 1) < length
        return jnp.where(live, value, 0.0)

    @pl.when(step == 0)
    def _():
        if n_cand:
            x_ref[0:L, :] = ch_ref[0]
        for k, q in enumerate(picks):
            x_ref[L * (n_cand + k) : L * (n_cand + k + 1), :] = rh_ref[q]
        if weights:
            row = lax.broadcasted_iota(jnp.int32, (16, L), 0)
            co_ref[L:, :] = jnp.zeros((16, D), jnp.bfloat16)
            ro_ref[len(picks) * L :, :] = jnp.zeros((16, D), jnp.bfloat16)
            w = token_weights(cid_ref[...], clen_ref[0])
            count = jnp.full((1, 2 * SLOTS), count_ref[0], jnp.int32)
            slots = jnp.concatenate([pc_ref[...], pr_ref[...], count], axis=1).astype(jnp.float32)
            words = jnp.where(row == 0, w, jnp.where(row == 1, slots, 0.0))
            co_ref[L:, 0:L] = words.astype(jnp.bfloat16)
            block = jnp.zeros((16, L), jnp.float32)
            for q in range(4):
                block = jnp.where(row == q, token_weights(rid_ref[q : q + 1, :], rlen_ref[q]), block)
            ro_ref[len(picks) * L :, 0:L] = block.astype(jnp.bfloat16)

    w = up.shape[1] // sub
    x = x_ref[...]
    pre = [
        jnp.dot(x, up[:, k * w : (k + 1) * w], preferred_element_type=jnp.float32)
        + upb[:, k * w : (k + 1) * w]
        for k in range(sub)
    ]
    part = None
    for k in range(sub):
        h = pre[k]
        act = (0.5 * h * (lax.erf(h * 0.7071067811865476) + 1.0)).astype(jnp.bfloat16)
        d = jnp.dot(act, dn[k * w : (k + 1) * w, :], preferred_element_type=jnp.float32)
        part = d if part is None else part + d

    @pl.when(step == 0)
    def _():
        acc_ref[...] = part

    @pl.when(step > 0)
    def _():
        acc_ref[...] += part

    @pl.when(step == pl.num_programs(0) - 1)
    def _():
        for c in range(0, seqs * L, 64):
            r = slice(c, c + 64)
            s = x_ref[r, :].astype(jnp.float32) + acc_ref[r, :] + dnb[...]
            center = jnp.mean(s, axis=-1, keepdims=True)
            e = s - center
            spread = jnp.mean(e * e, axis=-1, keepdims=True)
            y = e * lax.rsqrt(spread + 1e-5) * gain[...] + bias[...]
            m = jnp.sum(y * y, axis=-1, keepdims=True)
            unit = (y * lax.rsqrt(m + 1e-6)).astype(jnp.bfloat16)
            if c < L * n_cand:
                co_ref[r, :] = unit
            else:
                ro_ref[c - L * n_cand : c - L * n_cand + 64, :] = unit


def encode(picks, cand, rh, words, layer, f=1024, sub=4):
    def full(a):
        return pl.BlockSpec(a.shape, lambda i: (0,) * a.ndim, pipeline_mode=pl.Buffered(1))

    up, upb, dn, dnb, gain, bias = layer
    n_cand = 0 if cand is None else 1
    extra = 16 if words else 0
    seqs = n_cand + len(picks)
    smem = pl.BlockSpec(memory_space=pltpu.SMEM)
    outs = [jax.ShapeDtypeStruct((L + extra, D), jnp.bfloat16)] * n_cand + [
        jax.ShapeDtypeStruct((len(picks) * L + extra, D), jnp.bfloat16)
    ]
    first = list(words) + ([cand] if n_cand else []) + [rh]
    return pl.pallas_call(
        functools.partial(encode_kernel, n_cand, picks, bool(words), sub),
        grid=(up.shape[1] // f,),
        in_specs=[smem if k < 3 and words else full(a) for k, a in enumerate(first)]
        + [
            pl.BlockSpec((D, f), lambda i: (0, i)),
            pl.BlockSpec((1, f), lambda i: (0, i)),
            pl.BlockSpec((f, D), lambda i: (i, 0)),
            full(dnb),
            full(gain),
            full(bias),
        ],
        out_specs=[pl.BlockSpec(o.shape, lambda i: (0, 0)) for o in outs],
        out_shape=outs,
        scratch_shapes=[
            pltpu.VMEM((seqs * L, D), jnp.bfloat16),
            pltpu.VMEM((seqs * L, D), jnp.float32),
        ],
        compiler_params=pltpu.CompilerParams(
            dimension_semantics=("arbitrary",), vmem_limit_bytes=60 << 20
        ),
        cost_estimate=pl.CostEstimate(
            flops=4 * seqs * L * D * up.shape[1], bytes_accessed=17 << 20, transcendentals=0
        ),
        name="encode",
    )(*first, up, upb, dn, dnb, gain, bias)


GROUP = 4


def score_listed(todo, n, acc, total, cands, refs, cbuf, rbuf, wbuf, sem):
    def start(t, b):
        for k, buf in enumerate(cands):
            @pl.when(todo[0, t] == k)
            def _():
                pltpu.make_async_copy(buf.at[todo[1, t]], cbuf.at[b], sem.at[0, b]).start()
        at = pl.multiple_of(todo[3, t] * L, L)
        for k, buf in enumerate(refs):
            @pl.when(todo[2, t] == k)
            def _():
                words = refs[k - k % 2]
                pltpu.make_async_copy(buf.at[pl.ds(at, L), :], rbuf.at[b], sem.at[1, b]).start()
                pltpu.make_async_copy(
                    words.at[pl.ds(2 * L, 16), pl.ds(0, L)], wbuf.at[b], sem.at[2, b]
                ).start()

    def start_group(g):
        for k in range(GROUP):
            t = g * GROUP + k

            @pl.when(t < n)
            def _(t=t, k=k):
                start(t, (g % 2) * GROUP + k)

    start_group(0)
    lane = lax.broadcasted_iota(jnp.int32, (8, L), 1)
    sub = lax.broadcasted_iota(jnp.int32, (8, L), 0)
    eye = lax.broadcasted_iota(jnp.int32, (L, L), 0) == lax.broadcasted_iota(jnp.int32, (L, L), 1)

    def one(t, b):
        similar = lax.dot_general(
            cbuf[b, 0:L, :], rbuf[b], (((1,), (1,)), ((), ())), preferred_element_type=jnp.float32
        )
        cw = cbuf[b, L:, 0:L].astype(jnp.float32)[0:1, :]
        wide = wbuf[b].astype(jnp.float32)
        rsub = lax.broadcasted_iota(jnp.int32, (16, L), 0)
        rw = jnp.sum(jnp.where(rsub == todo[4, t], wide, 0.0), axis=0, keepdims=True)
        cw_col = jnp.sum(jnp.where(eye, cw, 0.0), axis=1, keepdims=True)
        row_best = jnp.max(jnp.where(rw > 0, similar, -10000.0), axis=1, keepdims=True)
        col_best = jnp.max(jnp.where(cw_col > 0, similar, -10000.0), axis=0, keepdims=True)
        precision = jnp.sum(cw_col * row_best, axis=0, keepdims=True) / jnp.sum(
            cw, axis=1, keepdims=True
        )
        recall = jnp.sum(rw * col_best, axis=1, keepdims=True) / jnp.sum(rw, axis=1, keepdims=True)
        fmeasure = 2.0 * precision * recall / jnp.maximum(precision + recall, 0.7)
        return precision, recall, fmeasure

    def group(g, carry):
        acc, total = carry
        start_group(g + 1)
        for k in range(GROUP):
            b = (g % 2) * GROUP + k

            @pl.when(g * GROUP + k < n)
            def _(b=b):
                pltpu.make_async_copy(cands[0].at[0], cbuf.at[b], sem.at[0, b]).wait()
                pltpu.make_async_copy(refs[0].at[pl.ds(0, L), :], rbuf.at[b], sem.at[1, b]).wait()
                pltpu.make_async_copy(
                    refs[0].at[pl.ds(2 * L, 16), pl.ds(0, L)], wbuf.at[b], sem.at[2, b]
                ).wait()

        scores = []
        for k in range(GROUP):
            t = jnp.minimum(g * GROUP + k, n - 1)
            scores.append((t, g * GROUP + k < n, one(t, (g % 2) * GROUP + k)))
        for t, real, (p, r, f) in scores:
            three = jnp.where(lane < 32, p, jnp.where(lane < 64, r, f))
            here = (sub == todo[5, t]) & ((lane & 31) == todo[6, t]) & (lane < 96) & real
            acc = jnp.where(here, three, acc)
            rows = jnp.where(sub == 0, p, jnp.where(sub == 1, r, f))
            total = total + jnp.where(real, rows, 0.0)
        return acc, total

    return lax.fori_loop(0, (n + GROUP - 1) // GROUP, group, (acc, total))


def early_kernel(pos_ref, *refs):
    cands, refs_, refs = refs[:10], refs[10:16], refs[16:]
    out_ref, later, cbuf, rbuf, wbuf, todo, lbuf, lint, lists, lsem, sem = refs
    y, core, x, z = pos_ref[0], pos_ref[1], pos_ref[2], pos_ref[3]

    for own, places in ((0, ((0, 0), (1, 0), (2, 0), (3, 0))), (1, ((0, 0), (0, 1), (0, 3), (0, 2)))):
        @pl.when(core == own)
        def _(places=places):
            for k, (buf, row) in enumerate(places):
                words = cands[buf].at[row, pl.ds(L, 16), pl.ds(0, L)]
                pltpu.make_async_copy(words, lbuf.at[k], lsem.at[k]).start()

    for k in range(4):
        words = cands[0].at[0, pl.ds(L, 16), pl.ds(0, L)]
        pltpu.make_async_copy(words, lbuf.at[k], lsem.at[k]).wait()
        lint[k : k + 1, :] = lbuf[k].astype(jnp.float32)[1:2, :].astype(jnp.int32)
    move = pltpu.make_async_copy(lint, lists, lsem.at[0])
    move.start()
    move.wait()
    n = m = jnp.int32(0)
    for k, dz in enumerate((0, 3, 1, 2)):
        zj = (z + dz) & 3

        def scan(s, counts, k=k, dz=dz, zj=zj):
            n, m = counts
            c = lists[k, s]
            r = lists[k, SLOTS + s]
            mine = (r & 3) == z
            dx = (((r & 15) >> 2) - x) & 3
            late = mine & (dx == 2)
            soon = mine & (dx != 2)
            kc = c & 1
            dy = ((c >> 1) - y) & 3
            u1 = jnp.where(kc == 0, dy, dz)
            u2 = jnp.where(kc == 0, dz, dy)
            i1 = (4 - u1) & 3
            g2 = (u2 == 3) * 1 + (u2 == 1) * 2 + (u2 == 2) * 3
            g2 = jnp.where((g2 == 3) & (i1 >= 2), 4, g2)
            src = g2 + jnp.where(kc == core, 0, 5)
            row = jnp.where(g2 == 4, i1 - 2, i1)
            i = r >> 4
            back = jnp.where(core == 0, 3, 1)
            rs = jnp.where(dx == 0, 0, jnp.where(dx == 2, 3, jnp.where(dx == back, 1, 2)))

            def put(where, at, rs):
                where[0, at] = src
                where[1, at] = row
                where[2, at] = rs * 2 + (i >> 1)
                where[3, at] = i & 1
                where[4, at] = i
                where[5, at] = zj
                where[6, at] = s

            @pl.when(soon)
            def _():
                put(todo, n, rs)

            @pl.when(late)
            def _():
                put(later, m, 0)

            return n + jnp.where(soon, 1, 0), m + jnp.where(late, 1, 0)

        n, m = lax.fori_loop(0, lists[k, 2 * SLOTS], scan, (n, m))
    later[7, 0] = m
    zero = jnp.zeros((8, L), jnp.float32)
    acc, total = score_listed(todo, n, zero, zero, cands, refs_, cbuf, rbuf, wbuf, sem)
    out_ref[0] = acc
    out_ref[1] = total


def late_kernel(pos_ref, count_ref, todo, *refs):
    cands, refs_, (part, out_ref, cbuf, rbuf, wbuf, sem) = refs[:10], refs[10:12], refs[12:]
    y, core, x = pos_ref[0], pos_ref[1], pos_ref[2]
    acc, total = score_listed(todo, todo[7, 0], part[0], part[1], cands, refs_, cbuf, rbuf, wbuf, sem)
    lane = lax.broadcasted_iota(jnp.int32, (1, L), 1)
    count = count_ref[0].astype(jnp.float32)
    sums = jnp.where(
        lane == 96,
        total[0:1, :],
        jnp.where(lane == 97, total[1:2, :], jnp.where(lane == 98, total[2:3, :], count)),
    )
    sums = jnp.where((lane >= 96) & (lane < 100), sums, 0.0)
    for q in range(out_ref.shape[0]):
        out_ref[q] = sums
    mine = (y * 2 + core) * 4 + x
    for q in range(4):
        out_ref[mine * 4 + q] = acc[q : q + 1, :] + sums


def finish_kernel(got_ref, scores_ref, totals_ref):
    s = jnp.sum(got_ref[...], axis=0)
    for k in range(3):
        scores_ref[k, 0] = s[:, k * SLOTS : (k + 1) * SLOTS]
    totals_ref[...] = s[:, 96:99] / s[:, 99:100]


def pair_call(kernel, name, cost, smem_args, hbm_args, vmem_args, out_specs, out_shape, scratch):
    smem = pl.BlockSpec(memory_space=pltpu.SMEM)
    hbm = pl.BlockSpec(memory_space=pl.ANY)
    vmem = pl.BlockSpec(memory_space=pltpu.VMEM)
    return pl.pallas_call(
        kernel,
        in_specs=[smem] * len(smem_args) + [hbm] * len(hbm_args) + [vmem] * len(vmem_args),
        out_specs=out_specs,
        out_shape=out_shape,
        scratch_shapes=[
            pltpu.VMEM((2 * GROUP, L + 16, D), jnp.bfloat16),
            pltpu.VMEM((2 * GROUP, L, D), jnp.bfloat16),
            pltpu.VMEM((2 * GROUP, 16, L), jnp.bfloat16),
            *scratch,
            pltpu.SemaphoreType.DMA((3, 2 * GROUP)),
        ],
        compiler_params=pltpu.CompilerParams(vmem_limit_bytes=12 << 20),
        cost_estimate=pl.CostEstimate(
            flops=cost << 10, bytes_accessed=cost, transcendentals=0
        ),
        name=name,
    )(*smem_args, *hbm_args, *vmem_args)


def on_device(
    cand_hidden, ref_hidden, cand_ids, ref_ids, cand_len, reference_length, idf_table, up_weight,
    up_bias, down_weight, down_bias, norm_gain, norm_bias, pair_cand, pair_ref, pair_count,
):
    table = jnp.pad(idf_table, (0, TABLE_ROWS * 128 - idf_table.shape[0])).reshape(TABLE_ROWS, 128)
    count = pair_count.reshape(1)
    dp, prompt = lax.axis_index("dp"), lax.axis_index("prompt")
    pos = jnp.stack([dp >> 1, dp & 1, prompt >> 2, prompt & 3]).astype(jnp.int32)
    layer = (
        up_weight,
        up_bias.reshape(1, -1),
        down_weight,
        down_bias.reshape(1, -1),
        norm_gain.reshape(1, -1),
        norm_bias.reshape(1, -1),
    )
    hidden = ref_hidden.reshape(4, L, D)
    words = (
        cand_len.reshape(1),
        reference_length.reshape(4),
        count,
        cand_ids.reshape(1, L),
        ref_ids.reshape(4, L),
        pair_cand.reshape(1, SLOTS),
        pair_ref.reshape(1, SLOTS),
        table,
    )
    cand, refs_a = encode((0, 1), cand_hidden.reshape(1, L, D), hidden, words, layer)
    back_a = send(refs_a, along_x(1))
    ahead_a = send(refs_a, along_x(-1))
    c1 = send(cand, along_first(1))
    c3 = send(cand, along_first(-1))
    c2 = send(cand, along_first(2))
    (refs_b,) = encode((2, 3), None, hidden, (), layer)
    back_a, ahead_a, c1, c2, c3, refs_b, pos = lax.optimization_barrier(
        (back_a, ahead_a, c1, c2, c3, refs_b, pos)
    )
    back_b = send(refs_b, along_x(1))
    ahead_b = send(refs_b, along_x(-1))
    far_a = send(back_a, along_x(1))
    own4 = jnp.stack([cand, c1, c2, c3])
    d1 = send(own4, along_second(1))
    d2 = send(own4, along_second(-1))
    d3 = send(d1[:2], along_second(1))
    d4 = send(d2[2:], along_second(-1))
    d3, d4, far_a, back_b, ahead_b = lax.optimization_barrier((d3, d4, far_a, back_b, ahead_b))
    far_b = send(back_b, along_x(1))
    others = [send(v, to_other_core) for v in (own4, d1, d2, d3, d4)]
    cands = [own4, d1, d2, d3, d4, *others]
    part, later = pair_call(
        early_kernel,
        "score_early",
        1 << 10,
        [pos],
        [*cands, refs_a, refs_b, back_a, back_b, ahead_a, ahead_b],
        [],
        [pl.BlockSpec(memory_space=pltpu.VMEM), pl.BlockSpec(memory_space=pltpu.SMEM)],
        [
            jax.ShapeDtypeStruct((2, 8, L), jnp.float32),
            jax.ShapeDtypeStruct((8, 4 * SLOTS), jnp.int32),
        ],
        [
            pltpu.SMEM((8, 4 * SLOTS), jnp.int32),
            pltpu.VMEM((4, 16, L), jnp.bfloat16),
            pltpu.VMEM((8, L), jnp.int32),
            pltpu.SMEM((8, L), jnp.int32),
            pltpu.SemaphoreType.DMA((4,)),
        ],
    )
    payload = pair_call(
        late_kernel,
        "score_late",
        1 << 20,
        [pos, count, later],
        [*cands, far_a, far_b],
        [part],
        pl.BlockSpec(memory_space=pltpu.VMEM),
        jax.ShapeDtypeStruct((128, 1, L), jnp.float32),
        [],
    )
    got = lax.all_to_all(payload, AXES, 0, 0)
    scores, totals = pl.pallas_call(
        finish_kernel,
        out_shape=[
            jax.ShapeDtypeStruct((3, 1, 1, SLOTS), jnp.float32),
            jax.ShapeDtypeStruct((1, 3), jnp.float32),
        ],
        name="finish",
    )(got)
    return scores, totals.reshape(3)


def solution(mesh):
    placed = (
        P("prompt", "dp", None, None),
        P("dp", "prompt", None, None),
        P("prompt", "dp", None),
        P("dp", "prompt", None),
        P("prompt", "dp"),
        P("dp", "prompt"),
        P(),
        P(),
        P(),
        P(),
        P(),
        P(),
        P(),
        P("dp", "prompt", None),
        P("dp", "prompt", None),
        P("dp", "prompt"),
    )
    return jax.shard_map(
        on_device,
        mesh=mesh,
        in_specs=placed,
        out_specs=(P(None, "dp", "prompt", None), P()),
        check_vma=False,
    )
```

```python
import functools

import jax
import jax.numpy as jnp
from jax import lax
from jax.experimental import pallas as pl
from jax.experimental.pallas import tpu as pltpu
from jax.sharding import PartitionSpec as P

D = 1024
L = 128
SLOTS = 32
TABLE_ROWS = 400
AXES = ("dp", "prompt")
GRID = [(y, c, x, z) for y in range(4) for c in range(2) for x in range(4) for z in range(4)]


def number(y, c, x, z):
    return (((y % 4) * 2 + c) * 4 + x % 4) * 4 + z % 4


def send(value, where):
    return lax.ppermute(value, AXES, [(number(*a), number(*where(*a))) for a in GRID])


def along_x(step):
    return lambda y, c, x, z: (y, c, x + (step if c == 0 else -step), z)


def along_first(step):
    return lambda y, c, x, z: (y + step, c, x, z) if c == 0 else (y, c, x, z + step)


def along_second(step):
    return lambda y, c, x, z: (y, c, x, z + step) if c == 0 else (y + step, c, x, z)


def along_z(step):
    return lambda y, c, x, z: (y, c, x, z + step)


def to_other_core(y, c, x, z):
    return (y, 1 - c, x, z)


def encode_kernel(
    sub, clen_ref, rlen_ref, count_ref, cid_ref, rid_ref, pc_ref, pr_ref, tbl_ref, ch_ref, rh_ref,
    up, upb, dn, dnb, gain, bias, co_ref, ra_ref, rb_ref, x_ref, acc_ref,
):
    step = pl.program_id(0)

    def token_weights(ids, length):
        high, low = ids >> 7, ids & 127
        hot = (lax.broadcasted_iota(jnp.int32, (TABLE_ROWS, L), 0) == high).astype(jnp.bfloat16)
        rows = lax.dot_general(
            tbl_ref[...].astype(jnp.bfloat16), hot, (((0,), (0,)), ((), ())), preferred_element_type=jnp.float32
        )
        mine = lax.broadcasted_iota(jnp.int32, (128, L), 0) == low
        value = jnp.sum(jnp.where(mine, rows, 0.0), axis=0, keepdims=True)
        live = lax.broadcasted_iota(jnp.int32, (1, L), 1) < length
        return jnp.where(live, value, 0.0)

    @pl.when(step == 0)
    def _():
        x_ref[0:L, :] = ch_ref[0]
        for q in range(4):
            x_ref[L * (q + 1) : L * (q + 2), :] = rh_ref[q]
        if True:
            row = lax.broadcasted_iota(jnp.int32, (16, L), 0)
            co_ref[L:, :] = jnp.zeros((16, D), jnp.bfloat16)
            ra_ref[L:, :] = jnp.zeros((16, D), jnp.bfloat16)
            w = token_weights(cid_ref[...], clen_ref[0])
            count = jnp.full((1, 2 * SLOTS), count_ref[0], jnp.int32)
            slots = jnp.concatenate([pc_ref[...], pr_ref[...], count], axis=1).astype(jnp.float32)
            words = jnp.where(row == 0, w, jnp.where(row == 1, slots, 0.0))
            co_ref[L:, 0:L] = words.astype(jnp.bfloat16)
            block = jnp.zeros((16, L), jnp.float32)
            for q in range(4):
                block = jnp.where(row == q, token_weights(rid_ref[q : q + 1, :], rlen_ref[q]), block)
            ra_ref[L:, 0:L] = block.astype(jnp.bfloat16)

    w = up.shape[1] // sub
    x = x_ref[...]
    pre = [
        jnp.dot(x, up[:, k * w : (k + 1) * w], preferred_element_type=jnp.float32)
        + upb[:, k * w : (k + 1) * w]
        for k in range(sub)
    ]
    part = None
    for k in range(sub):
        h = pre[k]
        act = (0.5 * h * (lax.erf(h * 0.7071067811865476) + 1.0)).astype(jnp.bfloat16)
        d = jnp.dot(act, dn[k * w : (k + 1) * w, :], preferred_element_type=jnp.float32)
        part = d if part is None else part + d

    @pl.when(step == 0)
    def _():
        acc_ref[...] = part

    @pl.when(step > 0)
    def _():
        acc_ref[...] += part

    @pl.when(step == pl.num_programs(0) - 1)
    def _():
        for c in range(0, 5 * L, 64):
            r = slice(c, c + 64)
            s = x_ref[r, :].astype(jnp.float32) + acc_ref[r, :] + dnb[...]
            center = jnp.mean(s, axis=-1, keepdims=True)
            e = s - center
            spread = jnp.mean(e * e, axis=-1, keepdims=True)
            y = e * lax.rsqrt(spread + 1e-5) * gain[...] + bias[...]
            m = jnp.sum(y * y, axis=-1, keepdims=True)
            unit = (y * lax.rsqrt(m + 1e-6)).astype(jnp.bfloat16)
            if c < L:
                co_ref[r, :] = unit
            elif c < 2 * L:
                ra_ref[c - L : c - L + 64, :] = unit
            else:
                rb_ref[c - 2 * L : c - 2 * L + 64, :] = unit


def encode(words, cand, refs, layer, f=1024, sub=4):
    def full(a):
        return pl.BlockSpec(a.shape, lambda i: (0,) * a.ndim, pipeline_mode=pl.Buffered(1))

    up, upb, dn, dnb, gain, bias = layer
    smem = pl.BlockSpec(memory_space=pltpu.SMEM)
    outs = [jax.ShapeDtypeStruct((n, D), jnp.bfloat16) for n in (L + 16, L + 16, 3 * L)]
    first = [*words, cand, refs]
    return pl.pallas_call(
        functools.partial(encode_kernel, sub),
        grid=(up.shape[1] // f,),
        in_specs=[smem if k < 3 else full(a) for k, a in enumerate(first)]
        + [
            pl.BlockSpec((D, f), lambda i: (0, i)),
            pl.BlockSpec((1, f), lambda i: (0, i)),
            pl.BlockSpec((f, D), lambda i: (i, 0)),
            full(dnb),
            full(gain),
            full(bias),
        ],
        out_specs=[pl.BlockSpec(o.shape, lambda i: (0, 0)) for o in outs],
        out_shape=outs,
        scratch_shapes=[pltpu.VMEM((5 * L, D), jnp.bfloat16), pltpu.VMEM((5 * L, D), jnp.float32)],
        compiler_params=pltpu.CompilerParams(
            dimension_semantics=("arbitrary",), vmem_limit_bytes=60 << 20
        ),
        name="encode",
    )(*first, up, upb, dn, dnb, gain, bias)


GROUP = 8


def pair_kernel(pos_ref, count_ref, *refs):
    cands, blocks, refs = refs[:10], refs[10:18], refs[18:]
    out_ref, cbuf, rbuf, wbuf, todo, lint, lists, lsem = refs
    y, core, x, z = pos_ref[0], pos_ref[1], pos_ref[2], pos_ref[3]

    for own, places in ((0, ((0, 0), (1, 0), (2, 0), (3, 0))), (1, ((0, 0), (0, 1), (0, 3), (0, 2)))):
        @pl.when(core == own)
        def _(places=places):
            for k, (buf, row) in enumerate(places):
                words = cands[buf][row, L : L + 16, 0:L].astype(jnp.float32)
                lint[k : k + 1, :] = words[1:2, :].astype(jnp.int32)

    move = pltpu.make_async_copy(lint, lists, lsem)
    move.start()
    move.wait()
    n = jnp.int32(0)
    for k, dz in enumerate((0, 3, 1, 2)):
        zj = (z + dz) & 3

        def scan(s, n, k=k, dz=dz, zj=zj):
            c = lists[k, s]
            r = lists[k, SLOTS + s]
            mine = (r & 3) == z

            @pl.when(mine)
            def _():
                dx = (((r & 15) >> 2) - x) & 3
                kc = c & 1
                dy = ((c >> 1) - y) & 3
                u1 = jnp.where(kc == 0, dy, dz)
                u2 = jnp.where(kc == 0, dz, dy)
                i1 = (4 - u1) & 3
                g2 = (u2 == 3) * 1 + (u2 == 1) * 2 + (u2 == 2) * 3
                g2 = jnp.where((g2 == 3) & (i1 >= 2), 4, g2)
                i = r >> 4
                back = jnp.where(core == 0, 3, 1)
                rs = jnp.where(dx == 0, 0, jnp.where(dx == 2, 3, jnp.where(dx == back, 1, 2)))
                todo[0, n] = g2 + jnp.where(kc == core, 0, 5)
                todo[1, n] = jnp.where(g2 == 4, i1 - 2, i1)
                todo[2, n] = rs * 2 + jnp.where(i == 0, 0, 1)
                todo[3, n] = jnp.maximum(i - 1, 0)
                todo[4, n] = i
                todo[5, n] = zj
                todo[6, n] = s

            return n + jnp.where(mine, 1, 0)

        n = lax.fori_loop(0, lists[k, 2 * SLOTS], scan, n)

    lane = lax.broadcasted_iota(jnp.int32, (8, L), 1)
    sub = lax.broadcasted_iota(jnp.int32, (8, L), 0)
    eye = lax.broadcasted_iota(jnp.int32, (L, L), 0) == lax.broadcasted_iota(jnp.int32, (L, L), 1)

    def fetch(t, b):
        for k, buf in enumerate(cands):
            @pl.when(todo[0, t] == k)
            def _(buf=buf):
                cbuf[b] = buf[todo[1, t]]
        for k, buf in enumerate(blocks):
            @pl.when(todo[2, t] == k)
            def _(k=k, buf=buf):
                if k % 2:
                    rbuf[b] = buf[pl.ds(pl.multiple_of(todo[3, t] * L, L), L), :]
                else:
                    rbuf[b] = buf[0:L, :]
                wbuf[b] = blocks[k - k % 2][L : L + 16, 0:L]

    def one(t, b):
        similar = lax.dot_general(
            cbuf[b, 0:L, :], rbuf[b], (((1,), (1,)), ((), ())), preferred_element_type=jnp.float32
        )
        cw = cbuf[b, L:, 0:L].astype(jnp.float32)[0:1, :]
        wide = wbuf[b].astype(jnp.float32)
        rsub = lax.broadcasted_iota(jnp.int32, (16, L), 0)
        rw = jnp.sum(jnp.where(rsub == todo[4, t], wide, 0.0), axis=0, keepdims=True)
        cw_col = jnp.sum(jnp.where(eye, cw, 0.0), axis=1, keepdims=True)
        row_best = jnp.max(jnp.where(rw > 0, similar, -10000.0), axis=1, keepdims=True)
        col_best = jnp.max(jnp.where(cw_col > 0, similar, -10000.0), axis=0, keepdims=True)
        precision = jnp.sum(cw_col * row_best, axis=0, keepdims=True) / jnp.sum(
            cw, axis=1, keepdims=True
        )
        recall = jnp.sum(rw * col_best, axis=1, keepdims=True) / jnp.sum(rw, axis=1, keepdims=True)
        fmeasure = 2.0 * precision * recall / jnp.maximum(precision + recall, 0.7)
        return precision, recall, fmeasure

    def group(g, carry):
        acc, total = carry
        for k in range(GROUP):
            t = g * GROUP + k

            @pl.when(t < n)
            def _(t=t, k=k):
                fetch(t, k)

        scores = []
        for k in range(GROUP):
            t = jnp.minimum(g * GROUP + k, n - 1)
            scores.append((t, g * GROUP + k < n, one(t, k)))
        for t, real, (p, r, f) in scores:
            three = jnp.where(lane < 32, p, jnp.where(lane < 64, r, f))
            here = (sub == todo[5, t]) & ((lane & 31) == todo[6, t]) & (lane < 96) & real
            acc = jnp.where(here, three, acc)
            rows = jnp.where(sub == 0, p, jnp.where(sub == 1, r, f))
            total = total + jnp.where(real, rows, 0.0)
        return acc, total

    zero = jnp.zeros((8, L), jnp.float32)
    acc, total = lax.fori_loop(0, (n + GROUP - 1) // GROUP, group, (zero, zero))
    line = lax.broadcasted_iota(jnp.int32, (1, L), 1)
    count = count_ref[0].astype(jnp.float32)
    sums = jnp.where(
        line == 96,
        total[0:1, :],
        jnp.where(line == 97, total[1:2, :], jnp.where(line == 98, total[2:3, :], count)),
    )
    sums = jnp.where((line >= 96) & (line < 100), sums, 0.0)
    out_ref[...] = jnp.broadcast_to(sums[None], out_ref.shape)
    mine = (y * 2 + core) * 4 + x
    for q in range(4):
        out_ref[mine * 4 + q] = acc[q : q + 1, :] + sums


def finish_kernel(got_ref, scores_ref, totals_ref):
    s = jnp.sum(got_ref[...], axis=0)
    for k in range(3):
        scores_ref[k, 0] = s[:, k * SLOTS : (k + 1) * SLOTS]
    totals_ref[...] = s[:, 96:99] / s[:, 99:100]


def score_pairs(pos, count, blocks):
    smem = pl.BlockSpec(memory_space=pltpu.SMEM)
    vmem = pl.BlockSpec(memory_space=pltpu.VMEM)
    return pl.pallas_call(
        pair_kernel,
        in_specs=[smem] * 2 + [vmem] * len(blocks),
        out_specs=vmem,
        out_shape=jax.ShapeDtypeStruct((128, 1, L), jnp.float32),
        scratch_shapes=[
            pltpu.VMEM((GROUP, L + 16, D), jnp.bfloat16),
            pltpu.VMEM((GROUP, L, D), jnp.bfloat16),
            pltpu.VMEM((GROUP, 16, L), jnp.bfloat16),
            pltpu.SMEM((8, 4 * SLOTS), jnp.int32),
            pltpu.VMEM((8, L), jnp.int32),
            pltpu.SMEM((8, L), jnp.int32),
            pltpu.SemaphoreType.DMA,
        ],
        compiler_params=pltpu.CompilerParams(vmem_limit_bytes=30 << 20),
        name="score_pairs",
    )(pos, count, *blocks)


def on_device(
    cand_hidden, ref_hidden, cand_ids, ref_ids, cand_len, reference_length, idf_table, up_weight,
    up_bias, down_weight, down_bias, norm_gain, norm_bias, pair_cand, pair_ref, pair_count,
):
    table = jnp.pad(idf_table, (0, TABLE_ROWS * 128 - idf_table.shape[0])).reshape(TABLE_ROWS, 128)
    count = pair_count.reshape(1)
    dp, prompt = lax.axis_index("dp"), lax.axis_index("prompt")
    pos = jnp.stack([dp >> 1, dp & 1, prompt >> 2, prompt & 3]).astype(jnp.int32)
    layer = (
        up_weight,
        up_bias.reshape(1, -1),
        down_weight,
        down_bias.reshape(1, -1),
        norm_gain.reshape(1, -1),
        norm_bias.reshape(1, -1),
    )
    hidden = ref_hidden.reshape(4, L, D)
    words = (
        cand_len.reshape(1),
        reference_length.reshape(4),
        count,
        cand_ids.reshape(1, L),
        ref_ids.reshape(4, L),
        pair_cand.reshape(1, SLOTS),
        pair_ref.reshape(1, SLOTS),
        table,
    )
    cand, refs_a, refs_b = encode(words, cand_hidden.reshape(1, L, D), hidden, layer)
    back_a = send(refs_a, along_x(1))
    ahead_a = send(refs_a, along_x(-1))
    c1 = send(cand, along_first(1))
    c3 = send(cand, along_first(-1))
    c2 = send(cand, along_first(2))
    back_a, ahead_a, c1, c2, c3, pos = lax.optimization_barrier((back_a, ahead_a, c1, c2, c3, pos))
    back_b = send(refs_b, along_x(1))
    ahead_b = send(refs_b, along_x(-1))
    far_a = send(back_a, along_x(1))
    own4 = jnp.stack([cand, c1, c2, c3])
    d1 = send(own4, along_second(1))
    d2 = send(own4, along_second(-1))
    d1, d2, back_b, ahead_b, far_a = lax.optimization_barrier((d1, d2, back_b, ahead_b, far_a))
    d3 = send(d1[:2], along_second(1))
    d4 = send(d2[2:], along_second(-1))
    far_b = send(back_b, along_x(1))
    d3, d4, far_b = lax.optimization_barrier((d3, d4, far_b))
    others = [send(v, to_other_core) for v in (own4, d1, d2, d3, d4)]
    cands = [own4, d1, d2, d3, d4, *others]
    blocks = [refs_a, refs_b, back_a, back_b, ahead_a, ahead_b, far_a, far_b]
    payload = score_pairs(pos, count, [*cands, *blocks])
    got = lax.all_to_all(payload, AXES, 0, 0)
    scores, totals = pl.pallas_call(
        finish_kernel,
        out_shape=[
            jax.ShapeDtypeStruct((3, 1, 1, SLOTS), jnp.float32),
            jax.ShapeDtypeStruct((1, 3), jnp.float32),
        ],
        name="finish",
    )(got)
    return scores, totals.reshape(3)


def solution(mesh):
    placed = (
        P("prompt", "dp", None, None),
        P("dp", "prompt", None, None),
        P("prompt", "dp", None),
        P("dp", "prompt", None),
        P("prompt", "dp"),
        P("dp", "prompt"),
        P(),
        P(),
        P(),
        P(),
        P(),
        P(),
        P(),
        P("dp", "prompt", None),
        P("dp", "prompt", None),
        P("dp", "prompt"),
    )
    return jax.shard_map(
        on_device,
        mesh=mesh,
        in_specs=placed,
        out_specs=(P(None, "dp", "prompt", None), P()),
        check_vma=False,
    )
```

```python
import functools

import jax
import jax.numpy as jnp
from jax import lax
from jax.experimental import pallas as pl
from jax.experimental.pallas import tpu as pltpu
from jax.sharding import PartitionSpec as P

D = 1024
L = 128
SLOTS = 32
TABLE_ROWS = 400
AXES = ("dp", "prompt")
GRID = [(y, c, x, z) for y in range(4) for c in range(2) for x in range(4) for z in range(4)]


def number(y, c, x, z):
    return (((y % 4) * 2 + c) * 4 + x % 4) * 4 + z % 4


def send(value, where):
    return lax.ppermute(value, AXES, [(number(*a), number(*where(*a))) for a in GRID])


def along_x(step):
    return lambda y, c, x, z: (y, c, x + (step if c == 0 else -step), z)


def along_first(step):
    return lambda y, c, x, z: (y + step, c, x, z) if c == 0 else (y, c, x, z + step)


def along_second(step):
    return lambda y, c, x, z: (y, c, x, z + step) if c == 0 else (y + step, c, x, z)


def along_z(step):
    return lambda y, c, x, z: (y, c, x, z + step)


def to_other_core(y, c, x, z):
    return (y, 1 - c, x, z)


def encode_kernel(n_cand, picks, weights, sub, *refs):
    refs = list(refs)
    if weights:
        clen_ref, rlen_ref, count_ref, cid_ref, rid_ref, pc_ref, pr_ref, tbl_ref = refs[:8]
        refs = refs[8:]
    ch_ref = refs.pop(0) if n_cand else None
    rh_ref, up, upb, dn, dnb, gain, bias = refs[:7]
    refs = refs[7:]
    co_ref = refs.pop(0) if n_cand else None
    ro_ref, x_ref, acc_ref = refs
    step = pl.program_id(0)
    seqs = n_cand + len(picks)

    def token_weights(ids, length):
        high, low = ids >> 7, ids & 127
        hot = (lax.broadcasted_iota(jnp.int32, (TABLE_ROWS, L), 0) == high).astype(jnp.bfloat16)
        rows = lax.dot_general(
            tbl_ref[...].astype(jnp.bfloat16), hot, (((0,), (0,)), ((), ())), preferred_element_type=jnp.float32
        )
        mine = lax.broadcasted_iota(jnp.int32, (128, L), 0) == low
        value = jnp.sum(jnp.where(mine, rows, 0.0), axis=0, keepdims=True)
        live = lax.broadcasted_iota(jnp.int32, (1, L), 1) < length
        return jnp.where(live, value, 0.0)

    @pl.when(step == 0)
    def _():
        if n_cand:
            x_ref[0:L, :] = ch_ref[0]
        for k, q in enumerate(picks):
            x_ref[L * (n_cand + k) : L * (n_cand + k + 1), :] = rh_ref[q]
        if weights:
            row = lax.broadcasted_iota(jnp.int32, (16, L), 0)
            co_ref[L:, :] = jnp.zeros((16, D), jnp.bfloat16)
            ro_ref[len(picks) * L :, :] = jnp.zeros((16, D), jnp.bfloat16)
            w = token_weights(cid_ref[...], clen_ref[0])
            count = jnp.full((1, 2 * SLOTS), count_ref[0], jnp.int32)
            slots = jnp.concatenate([pc_ref[...], pr_ref[...], count], axis=1).astype(jnp.float32)
            words = jnp.where(row == 0, w, jnp.where(row == 1, slots, 0.0))
            co_ref[L:, 0:L] = words.astype(jnp.bfloat16)
            block = jnp.zeros((16, L), jnp.float32)
            for q in range(4):
                block = jnp.where(row == q, token_weights(rid_ref[q : q + 1, :], rlen_ref[q]), block)
            ro_ref[len(picks) * L :, 0:L] = block.astype(jnp.bfloat16)

    w = up.shape[1] // sub
    x = x_ref[...]
    pre = [
        jnp.dot(x, up[:, k * w : (k + 1) * w], preferred_element_type=jnp.float32)
        + upb[:, k * w : (k + 1) * w]
        for k in range(sub)
    ]
    part = None
    for k in range(sub):
        h = pre[k]
        act = (0.5 * h * (lax.erf(h * 0.7071067811865476) + 1.0)).astype(jnp.bfloat16)
        d = jnp.dot(act, dn[k * w : (k + 1) * w, :], preferred_element_type=jnp.float32)
        part = d if part is None else part + d

    @pl.when(step == 0)
    def _():
        acc_ref[...] = part

    @pl.when(step > 0)
    def _():
        acc_ref[...] += part

    @pl.when(step == pl.num_programs(0) - 1)
    def _():
        for c in range(0, seqs * L, 64):
            r = slice(c, c + 64)
            s = x_ref[r, :].astype(jnp.float32) + acc_ref[r, :] + dnb[...]
            center = jnp.mean(s, axis=-1, keepdims=True)
            e = s - center
            spread = jnp.mean(e * e, axis=-1, keepdims=True)
            y = e * lax.rsqrt(spread + 1e-5) * gain[...] + bias[...]
            m = jnp.sum(y * y, axis=-1, keepdims=True)
            unit = (y * lax.rsqrt(m + 1e-6)).astype(jnp.bfloat16)
            if c < L * n_cand:
                co_ref[r, :] = unit
            else:
                ro_ref[c - L * n_cand : c - L * n_cand + 64, :] = unit


def encode(picks, cand, rh, words, layer, f=1024, sub=4):
    def full(a):
        return pl.BlockSpec(a.shape, lambda i: (0,) * a.ndim, pipeline_mode=pl.Buffered(1))

    up, upb, dn, dnb, gain, bias = layer
    n_cand = 0 if cand is None else 1
    extra = 16 if words else 0
    seqs = n_cand + len(picks)
    smem = pl.BlockSpec(memory_space=pltpu.SMEM)
    outs = [jax.ShapeDtypeStruct((L + extra, D), jnp.bfloat16)] * n_cand + [
        jax.ShapeDtypeStruct((len(picks) * L + extra, D), jnp.bfloat16)
    ]
    first = list(words) + ([cand] if n_cand else []) + [rh]
    return pl.pallas_call(
        functools.partial(encode_kernel, n_cand, picks, bool(words), sub),
        grid=(up.shape[1] // f,),
        in_specs=[smem if k < 3 and words else full(a) for k, a in enumerate(first)]
        + [
            pl.BlockSpec((D, f), lambda i: (0, i)),
            pl.BlockSpec((1, f), lambda i: (0, i)),
            pl.BlockSpec((f, D), lambda i: (i, 0)),
            full(dnb),
            full(gain),
            full(bias),
        ],
        out_specs=[pl.BlockSpec(o.shape, lambda i: (0, 0)) for o in outs],
        out_shape=outs,
        scratch_shapes=[
            pltpu.VMEM((seqs * L, D), jnp.bfloat16),
            pltpu.VMEM((seqs * L, D), jnp.float32),
        ],
        compiler_params=pltpu.CompilerParams(
            dimension_semantics=("arbitrary",), vmem_limit_bytes=60 << 20
        ),
        cost_estimate=pl.CostEstimate(
            flops=4 * seqs * L * D * up.shape[1], bytes_accessed=17 << 20, transcendentals=0
        ),
        name="encode",
    )(*first, up, upb, dn, dnb, gain, bias)


GROUP = 8
AHEAD = 3


def pair_kernel(pos_ref, count_ref, *refs):
    cands, blocks, refs = refs[:10], refs[10:18], refs[18:]
    out_ref, cbuf, rbuf, wbuf, todo, lint, lists, lsem = refs
    y, core, x, z = pos_ref[0], pos_ref[1], pos_ref[2], pos_ref[3]

    lint[...] = jnp.zeros((8, L), jnp.int32)
    for own, places in ((0, ((0, 0), (1, 0), (2, 0), (3, 0))), (1, ((0, 0), (0, 1), (0, 3), (0, 2)))):
        @pl.when(core == own)
        def _(places=places):
            for k, (buf, row) in enumerate(places):
                words = cands[buf][row, L : L + 16, 0:L].astype(jnp.float32)
                lint[k : k + 1, :] = words[1:2, :].astype(jnp.int32)

    lane = lax.broadcasted_iota(jnp.int32, (8, L), 1)
    sub = lax.broadcasted_iota(jnp.int32, (8, L), 0)
    c = lint[...]
    r = pltpu.roll(c, L - SLOTS, 1)
    live = (lane < SLOTS) & (lane < pltpu.roll(c, 2 * SLOTS, 1)) & ((r & 3) == z)
    dz = jnp.where(sub == 1, 3, jnp.where(sub == 2, 1, jnp.where(sub == 3, 2, 0)))
    dx = (((r & 15) >> 2) - x) & 3
    dy = ((c >> 1) - y) & 3
    even = (c & 1) == 0
    u1 = jnp.where(even, dy, dz)
    u2 = jnp.where(even, dz, dy)
    i1 = (4 - u1) & 3
    g2 = jnp.where(u2 == 3, 1, jnp.where(u2 == 1, 2, jnp.where(u2 == 2, jnp.where(i1 >= 2, 4, 3), 0)))
    source = g2 + jnp.where((c & 1) == core, 0, 5)
    row = jnp.where(g2 == 4, i1 - 2, i1)
    back = jnp.where(core == 0, 3, 1)
    rs = jnp.where(dx == 0, 0, jnp.where(dx == 2, 3, jnp.where(dx == back, 1, 2)))
    i = (r >> 4) & 3
    code = source | (row << 4) | (rs << 6) | (i << 8) | (((z + dz) & 3) << 10) | (lane << 12)
    lint[...] = jnp.where(live, code, -1)
    move = pltpu.make_async_copy(lint, lists, lsem)
    move.start()
    move.wait()

    def scan(s, n):
        for k in range(4):
            v = lists[k, s]
            todo[n] = v
            n = n + jnp.where(v >= 0, 1, 0)
        return n

    n = lax.fori_loop(0, SLOTS, scan, jnp.int32(0))
    eye = lax.broadcasted_iota(jnp.int32, (L, L), 0) == lax.broadcasted_iota(jnp.int32, (L, L), 1)

    def choose(v, low, high, act):
        if high - low == 1:
            act(low)
            return
        middle = (low + high) // 2

        @pl.when(v < middle)
        def _():
            choose(v, low, middle, act)

        @pl.when(v >= middle)
        def _():
            choose(v, middle, high, act)

    def fetch(t, b):
        code = todo[t]
        row = (code >> 4) & 3
        i = (code >> 8) & 3
        at = pl.multiple_of(jnp.where(i < AHEAD, i, i - AHEAD) * L, L)

        def take_cand(k):
            cbuf[b] = cands[k][row]

        def take_ref(k):
            rbuf[b] = blocks[k][pl.ds(at, L), :]
            wbuf[b] = blocks[k - k % 2][AHEAD * L : AHEAD * L + 16, 0:L]

        choose(code & 15, 0, 10, take_cand)
        choose(((code >> 6) & 3) * 2 + jnp.where(i < AHEAD, 0, 1), 0, 8, take_ref)

    def one(t, b):
        similar = lax.dot_general(
            cbuf[b, 0:L, :], rbuf[b], (((1,), (1,)), ((), ())), preferred_element_type=jnp.float32
        )
        cw = cbuf[b, L:, 0:L].astype(jnp.float32)[0:1, :]
        wide = wbuf[b].astype(jnp.float32)
        rsub = lax.broadcasted_iota(jnp.int32, (16, L), 0)
        rw = jnp.sum(jnp.where(rsub == ((todo[t] >> 8) & 3), wide, 0.0), axis=0, keepdims=True)
        cw_col = jnp.sum(jnp.where(eye, cw, 0.0), axis=1, keepdims=True)
        row_best = jnp.max(jnp.where(rw > 0, similar, -10000.0), axis=1, keepdims=True)
        col_best = jnp.max(jnp.where(cw_col > 0, similar, -10000.0), axis=0, keepdims=True)
        precision = jnp.sum(cw_col * row_best, axis=0, keepdims=True) / jnp.sum(
            cw, axis=1, keepdims=True
        )
        recall = jnp.sum(rw * col_best, axis=1, keepdims=True) / jnp.sum(rw, axis=1, keepdims=True)
        fmeasure = 2.0 * precision * recall / jnp.maximum(precision + recall, 0.7)
        return precision, recall, fmeasure

    def group(g, carry):
        acc, total = carry
        for k in range(GROUP):
            t = g * GROUP + k

            @pl.when(t < n)
            def _(t=t, k=k):
                fetch(t, k)

        scores = []
        for k in range(GROUP):
            t = g * GROUP + k
            scores.append((t, g * GROUP + k < n, one(t, k)))
        for t, real, (p, r, f) in scores:
            three = jnp.where(lane < 32, p, jnp.where(lane < 64, r, f))
            here = (sub == ((todo[t] >> 10) & 3)) & ((lane & 31) == ((todo[t] >> 12) & 31)) & (lane < 96) & real
            acc = jnp.where(here, three, acc)
            rows = jnp.where(sub == 0, p, jnp.where(sub == 1, r, f))
            total = total + jnp.where(real, rows, 0.0)
        return acc, total

    zero = jnp.zeros((8, L), jnp.float32)
    acc, total = lax.fori_loop(0, (n + GROUP - 1) // GROUP, group, (zero, zero))
    line = lax.broadcasted_iota(jnp.int32, (1, L), 1)
    count = count_ref[0].astype(jnp.float32)
    sums = jnp.where(
        line == 96,
        total[0:1, :],
        jnp.where(line == 97, total[1:2, :], jnp.where(line == 98, total[2:3, :], count)),
    )
    sums = jnp.where((line >= 96) & (line < 100), sums, 0.0)
    out_ref[...] = jnp.broadcast_to(sums[None], out_ref.shape)
    mine = (y * 2 + core) * 4 + x
    for q in range(4):
        out_ref[mine * 4 + q] = acc[q : q + 1, :] + sums


def finish_kernel(got_ref, scores_ref, totals_ref):
    s = jnp.sum(got_ref[...], axis=0)
    for k in range(3):
        scores_ref[k, 0] = s[:, k * SLOTS : (k + 1) * SLOTS]
    totals_ref[...] = s[:, 96:99] / s[:, 99:100]


def score_pairs(pos, count, blocks):
    smem = pl.BlockSpec(memory_space=pltpu.SMEM)
    vmem = pl.BlockSpec(memory_space=pltpu.VMEM)
    return pl.pallas_call(
        pair_kernel,
        in_specs=[smem] * 2 + [vmem] * len(blocks),
        out_specs=vmem,
        out_shape=jax.ShapeDtypeStruct((128, 1, L), jnp.float32),
        scratch_shapes=[
            pltpu.VMEM((GROUP, L + 16, D), jnp.bfloat16),
            pltpu.VMEM((GROUP, L, D), jnp.bfloat16),
            pltpu.VMEM((GROUP, 16, L), jnp.bfloat16),
            pltpu.SMEM((4 * SLOTS + GROUP,), jnp.int32),
            pltpu.VMEM((8, L), jnp.int32),
            pltpu.SMEM((8, L), jnp.int32),
            pltpu.SemaphoreType.DMA,
        ],
        compiler_params=pltpu.CompilerParams(vmem_limit_bytes=30 << 20),
        name="score_pairs",
    )(pos, count, *blocks)


def on_device(
    cand_hidden, ref_hidden, cand_ids, ref_ids, cand_len, reference_length, idf_table, up_weight,
    up_bias, down_weight, down_bias, norm_gain, norm_bias, pair_cand, pair_ref, pair_count,
):
    table = jnp.pad(idf_table, (0, TABLE_ROWS * 128 - idf_table.shape[0])).reshape(TABLE_ROWS, 128)
    count = pair_count.reshape(1)
    dp, prompt = lax.axis_index("dp"), lax.axis_index("prompt")
    pos = jnp.stack([dp >> 1, dp & 1, prompt >> 2, prompt & 3]).astype(jnp.int32)
    layer = (
        up_weight,
        up_bias.reshape(1, -1),
        down_weight,
        down_bias.reshape(1, -1),
        norm_gain.reshape(1, -1),
        norm_bias.reshape(1, -1),
    )
    hidden = ref_hidden.reshape(4, L, D)
    words = (
        cand_len.reshape(1),
        reference_length.reshape(4),
        count,
        cand_ids.reshape(1, L),
        ref_ids.reshape(4, L),
        pair_cand.reshape(1, SLOTS),
        pair_ref.reshape(1, SLOTS),
        table,
    )
    cand, refs_a = encode((0, 1, 2), cand_hidden.reshape(1, L, D), hidden, words, layer)
    c1 = send(cand, along_first(1))
    c3 = send(cand, along_first(-1))
    c2 = send(cand, along_first(2))
    back_a = send(refs_a, along_x(1))
    ahead_a = send(refs_a, along_x(-1))
    c1, c2, c3, hidden, pos = lax.optimization_barrier((c1, c2, c3, hidden, pos))
    own4 = jnp.stack([cand, c1, c2, c3])
    d1 = send(own4, along_second(1))
    d2 = send(own4, along_second(-1))
    (refs_b,) = encode((3,), None, hidden, (), layer)
    back_a, ahead_a, refs_b = lax.optimization_barrier((back_a, ahead_a, refs_b))
    back_b = send(refs_b, along_x(1))
    ahead_b = send(refs_b, along_x(-1))
    far_a = send(back_a, along_x(1))
    d3 = send(d1[:2], along_second(1))
    d4 = send(d2[2:], along_second(-1))
    own4, d1, d2, back_b, ahead_b = lax.optimization_barrier((own4, d1, d2, back_b, ahead_b))
    far_b = send(back_b, along_x(1))
    others = [send(v, to_other_core) for v in (own4, d1, d2)]
    d3, d4, far_a, far_b = lax.optimization_barrier((d3, d4, far_a, far_b))
    others += [send(v, to_other_core) for v in (d3, d4)]
    cands = [own4, d1, d2, d3, d4, *others]
    blocks = [refs_a, refs_b, back_a, back_b, ahead_a, ahead_b, far_a, far_b]
    payload = score_pairs(pos, count, [*cands, *blocks])
    got = lax.all_to_all(payload, AXES, 0, 0)
    scores, totals = pl.pallas_call(
        finish_kernel,
        out_shape=[
            jax.ShapeDtypeStruct((3, 1, 1, SLOTS), jnp.float32),
            jax.ShapeDtypeStruct((1, 3), jnp.float32),
        ],
        name="finish",
    )(got)
    return scores, totals.reshape(3)


def solution(mesh):
    placed = (
        P("prompt", "dp", None, None),
        P("dp", "prompt", None, None),
        P("prompt", "dp", None),
        P("dp", "prompt", None),
        P("prompt", "dp"),
        P("dp", "prompt"),
        P(),
        P(),
        P(),
        P(),
        P(),
        P(),
        P(),
        P("dp", "prompt", None),
        P("dp", "prompt", None),
        P("dp", "prompt"),
    )
    return jax.shard_map(
        on_device,
        mesh=mesh,
        in_specs=placed,
        out_specs=(P(None, "dp", "prompt", None), P()),
        check_vma=False,
    )
```

```python
import functools

import jax
import jax.numpy as jnp
from jax import lax
from jax.experimental import pallas as pl
from jax.experimental.pallas import tpu as pltpu
from jax.sharding import PartitionSpec as P

D = 1024
L = 128
SLOTS = 32
TABLE_ROWS = 400
AXES = ("dp", "prompt")
GRID = [(y, c, x, z) for y in range(4) for c in range(2) for x in range(4) for z in range(4)]


def number(y, c, x, z):
    return (((y % 4) * 2 + c) * 4 + x % 4) * 4 + z % 4


def send(value, where):
    return lax.ppermute(value, AXES, [(number(*a), number(*where(*a))) for a in GRID])


def along_x(step):
    return lambda y, c, x, z: (y, c, x + (step if c == 0 else -step), z)


def along_first(step):
    return lambda y, c, x, z: (y + step, c, x, z) if c == 0 else (y, c, x, z + step)


def along_second(step):
    return lambda y, c, x, z: (y, c, x, z + step) if c == 0 else (y + step, c, x, z)


def along_z(step):
    return lambda y, c, x, z: (y, c, x, z + step)


def to_other_core(y, c, x, z):
    return (y, 1 - c, x, z)


def encode_kernel(n_cand, picks, weights, sub, *refs):
    refs = list(refs)
    if weights:
        clen_ref, rlen_ref, count_ref, cid_ref, rid_ref, pc_ref, pr_ref, tbl_ref = refs[:8]
        refs = refs[8:]
    ch_ref = refs.pop(0) if n_cand else None
    rh_ref, up, upb, dn, dnb, gain, bias = refs[:7]
    refs = refs[7:]
    co_ref = refs.pop(0) if n_cand else None
    ro_ref, x_ref, acc_ref = refs
    step = pl.program_id(0)
    seqs = n_cand + len(picks)

    def token_weights(ids, length):
        high, low = ids >> 7, ids & 127
        hot = (lax.broadcasted_iota(jnp.int32, (TABLE_ROWS, L), 0) == high).astype(jnp.bfloat16)
        rows = lax.dot_general(
            tbl_ref[...].astype(jnp.bfloat16), hot, (((0,), (0,)), ((), ())), preferred_element_type=jnp.float32
        )
        mine = lax.broadcasted_iota(jnp.int32, (128, L), 0) == low
        value = jnp.sum(jnp.where(mine, rows, 0.0), axis=0, keepdims=True)
        live = lax.broadcasted_iota(jnp.int32, (1, L), 1) < length
        return jnp.where(live, value, 0.0)

    @pl.when(step == 0)
    def _():
        if n_cand:
            x_ref[0:L, :] = ch_ref[0]
        for k, q in enumerate(picks):
            x_ref[L * (n_cand + k) : L * (n_cand + k + 1), :] = rh_ref[q]
        if weights:
            row = lax.broadcasted_iota(jnp.int32, (16, L), 0)
            co_ref[L:, :] = jnp.zeros((16, D), jnp.bfloat16)
            ro_ref[len(picks) * L :, :] = jnp.zeros((16, D), jnp.bfloat16)
            w = token_weights(cid_ref[...], clen_ref[0])
            count = jnp.full((1, 2 * SLOTS), count_ref[0], jnp.int32)
            slots = jnp.concatenate([pc_ref[...], pr_ref[...], count], axis=1).astype(jnp.float32)
            words = jnp.where(row == 0, w, jnp.where(row == 1, slots, 0.0))
            co_ref[L:, 0:L] = words.astype(jnp.bfloat16)
            block = jnp.zeros((16, L), jnp.float32)
            for q in range(4):
                block = jnp.where(row == q, token_weights(rid_ref[q : q + 1, :], rlen_ref[q]), block)
            ro_ref[len(picks) * L :, 0:L] = block.astype(jnp.bfloat16)

    w = up.shape[1] // sub
    x = x_ref[...]
    pre = [
        jnp.dot(x, up[:, k * w : (k + 1) * w], preferred_element_type=jnp.float32)
        + upb[:, k * w : (k + 1) * w]
        for k in range(sub)
    ]
    part = None
    for k in range(sub):
        h = pre[k]
        act = (0.5 * h * (lax.erf(h * 0.7071067811865476) + 1.0)).astype(jnp.bfloat16)
        d = jnp.dot(act, dn[k * w : (k + 1) * w, :], preferred_element_type=jnp.float32)
        part = d if part is None else part + d

    @pl.when(step == 0)
    def _():
        acc_ref[...] = part

    @pl.when(step > 0)
    def _():
        acc_ref[...] += part

    @pl.when(step == pl.num_programs(0) - 1)
    def _():
        for c in range(0, seqs * L, 64):
            r = slice(c, c + 64)
            s = x_ref[r, :].astype(jnp.float32) + acc_ref[r, :] + dnb[...]
            center = jnp.mean(s, axis=-1, keepdims=True)
            e = s - center
            spread = jnp.mean(e * e, axis=-1, keepdims=True)
            y = e * lax.rsqrt(spread + 1e-5) * gain[...] + bias[...]
            m = jnp.sum(y * y, axis=-1, keepdims=True)
            unit = (y * lax.rsqrt(m + 1e-6)).astype(jnp.bfloat16)
            if c < L * n_cand:
                co_ref[r, :] = unit
            else:
                ro_ref[c - L * n_cand : c - L * n_cand + 64, :] = unit


def encode(picks, cand, rh, words, layer, f=1024, sub=4):
    def full(a):
        return pl.BlockSpec(a.shape, lambda i: (0,) * a.ndim, pipeline_mode=pl.Buffered(1))

    up, upb, dn, dnb, gain, bias = layer
    n_cand = 0 if cand is None else 1
    extra = 16 if words else 0
    seqs = n_cand + len(picks)
    smem = pl.BlockSpec(memory_space=pltpu.SMEM)
    outs = [jax.ShapeDtypeStruct((L + extra, D), jnp.bfloat16)] * n_cand + [
        jax.ShapeDtypeStruct((len(picks) * L + extra, D), jnp.bfloat16)
    ]
    first = list(words) + ([cand] if n_cand else []) + [rh]
    return pl.pallas_call(
        functools.partial(encode_kernel, n_cand, picks, bool(words), sub),
        grid=(up.shape[1] // f,),
        in_specs=[smem if k < 3 and words else full(a) for k, a in enumerate(first)]
        + [
            pl.BlockSpec((D, f), lambda i: (0, i)),
            pl.BlockSpec((1, f), lambda i: (0, i)),
            pl.BlockSpec((f, D), lambda i: (i, 0)),
            full(dnb),
            full(gain),
            full(bias),
        ],
        out_specs=[pl.BlockSpec(o.shape, lambda i: (0, 0)) for o in outs],
        out_shape=outs,
        scratch_shapes=[
            pltpu.VMEM((seqs * L, D), jnp.bfloat16),
            pltpu.VMEM((seqs * L, D), jnp.float32),
        ],
        compiler_params=pltpu.CompilerParams(
            dimension_semantics=("arbitrary",), vmem_limit_bytes=60 << 20
        ),
        cost_estimate=pl.CostEstimate(
            flops=4 * seqs * L * D * up.shape[1], bytes_accessed=17 << 20, transcendentals=0
        ),
        name="encode",
    )(*first, up, upb, dn, dnb, gain, bias)


GROUP = 8
AHEAD = 3


def pair_kernel(pos_ref, count_ref, *refs):
    cands, blocks, refs = refs[:10], refs[10:18], refs[18:]
    out_ref, cbuf, rbuf, wbuf, todo, lint, lists, lsem = refs
    y, core, x, z = pos_ref[0], pos_ref[1], pos_ref[2], pos_ref[3]

    lint[...] = jnp.zeros((8, L), jnp.int32)
    for own, places in ((0, ((0, 0), (1, 0), (2, 0), (3, 0))), (1, ((0, 0), (0, 1), (0, 3), (0, 2)))):
        @pl.when(core == own)
        def _(places=places):
            for k, (buf, row) in enumerate(places):
                words = cands[buf][row, L : L + 16, 0:L].astype(jnp.float32)
                lint[k : k + 1, :] = words[1:2, :].astype(jnp.int32)

    lane = lax.broadcasted_iota(jnp.int32, (8, L), 1)
    sub = lax.broadcasted_iota(jnp.int32, (8, L), 0)
    c = lint[...]
    r = pltpu.roll(c, L - SLOTS, 1)
    live = (lane < SLOTS) & (lane < pltpu.roll(c, 2 * SLOTS, 1)) & ((r & 3) == z)
    dz = jnp.where(sub == 1, 3, jnp.where(sub == 2, 1, jnp.where(sub == 3, 2, 0)))
    dx = (((r & 15) >> 2) - x) & 3
    dy = ((c >> 1) - y) & 3
    even = (c & 1) == 0
    u1 = jnp.where(even, dy, dz)
    u2 = jnp.where(even, dz, dy)
    i1 = (4 - u1) & 3
    g2 = jnp.where(u2 == 3, 1, jnp.where(u2 == 1, 2, jnp.where(u2 == 2, jnp.where(i1 >= 2, 4, 3), 0)))
    source = g2 + jnp.where((c & 1) == core, 0, 5)
    row = jnp.where(g2 == 4, i1 - 2, i1)
    back = jnp.where(core == 0, 3, 1)
    rs = jnp.where(dx == 0, 0, jnp.where(dx == 2, 3, jnp.where(dx == back, 1, 2)))
    i = (r >> 4) & 3
    code = source | (row << 4) | (rs << 6) | (i << 8) | (((z + dz) & 3) << 10) | (lane << 12)
    lint[...] = jnp.where(live, code, -1)
    move = pltpu.make_async_copy(lint, lists, lsem)
    move.start()
    move.wait()

    def scan(s, n):
        for k in range(4):
            v = lists[k, s]
            todo[n] = v
            n = n + jnp.where(v >= 0, 1, 0)
        return n

    n = lax.fori_loop(0, SLOTS, scan, jnp.int32(0))
    eye = lax.broadcasted_iota(jnp.int32, (L, L), 0) == lax.broadcasted_iota(jnp.int32, (L, L), 1)

    def choose(v, low, high, act):
        if high - low == 1:
            act(low)
            return
        middle = (low + high) // 2

        @pl.when(v < middle)
        def _():
            choose(v, low, middle, act)

        @pl.when(v >= middle)
        def _():
            choose(v, middle, high, act)

    def fetch(t, b):
        code = todo[t]
        row = (code >> 4) & 3
        i = (code >> 8) & 3
        at = pl.multiple_of(jnp.where(i < AHEAD, i, i - AHEAD) * L, L)

        def take_cand(k):
            cbuf[b] = cands[k][row]

        def take_ref(k):
            rbuf[b] = blocks[k][pl.ds(at, L), :]
            wbuf[b] = blocks[k - k % 2][AHEAD * L : AHEAD * L + 16, 0:L]

        choose(code & 15, 0, 10, take_cand)
        choose(((code >> 6) & 3) * 2 + jnp.where(i < AHEAD, 0, 1), 0, 8, take_ref)

    def one(t, b):
        similar = lax.dot_general(
            cbuf[b, 0:L, :], rbuf[b], (((1,), (1,)), ((), ())), preferred_element_type=jnp.float32
        )
        cw = cbuf[b, L:, 0:L].astype(jnp.float32)[0:1, :]
        wide = wbuf[b].astype(jnp.float32)
        rsub = lax.broadcasted_iota(jnp.int32, (16, L), 0)
        rw = jnp.sum(jnp.where(rsub == ((todo[t] >> 8) & 3), wide, 0.0), axis=0, keepdims=True)
        cw_col = jnp.sum(jnp.where(eye, cw, 0.0), axis=1, keepdims=True)
        row_best = jnp.max(jnp.where(rw > 0, similar, -10000.0), axis=1, keepdims=True)
        col_best = jnp.max(jnp.where(cw_col > 0, similar, -10000.0), axis=0, keepdims=True)
        precision = jnp.sum(cw_col * row_best, axis=0, keepdims=True) / jnp.sum(
            cw, axis=1, keepdims=True
        )
        recall = jnp.sum(rw * col_best, axis=1, keepdims=True) / jnp.sum(rw, axis=1, keepdims=True)
        fmeasure = 2.0 * precision * recall / jnp.maximum(precision + recall, 0.7)
        return precision, recall, fmeasure

    def group(g, carry):
        acc, total = carry
        for k in range(GROUP):
            t = g * GROUP + k

            @pl.when(t < n)
            def _(t=t, k=k):
                fetch(t, k)

        scores = []
        for k in range(GROUP):
            t = g * GROUP + k
            scores.append((t, g * GROUP + k < n, one(t, k)))
        for t, real, (p, r, f) in scores:
            three = jnp.where(lane < 32, p, jnp.where(lane < 64, r, f))
            here = (sub == ((todo[t] >> 10) & 3)) & ((lane & 31) == ((todo[t] >> 12) & 31)) & (lane < 96) & real
            acc = jnp.where(here, three, acc)
            rows = jnp.where(sub == 0, p, jnp.where(sub == 1, r, f))
            total = total + jnp.where(real, rows, 0.0)
        return acc, total

    zero = jnp.zeros((8, L), jnp.float32)
    acc, total = lax.fori_loop(0, (n + GROUP - 1) // GROUP, group, (zero, zero))
    line = lax.broadcasted_iota(jnp.int32, (1, L), 1)
    count = count_ref[0].astype(jnp.float32)
    sums = jnp.where(
        line == 96,
        total[0:1, :],
        jnp.where(line == 97, total[1:2, :], jnp.where(line == 98, total[2:3, :], count)),
    )
    sums = jnp.where((line >= 96) & (line < 100), sums, 0.0)
    out_ref[...] = jnp.broadcast_to(sums[None], out_ref.shape)
    mine = (y * 2 + core) * 4 + x
    for q in range(4):
        out_ref[mine * 4 + q] = acc[q : q + 1, :] + sums


def finish_kernel(got_ref, scores_ref, totals_ref):
    s = jnp.sum(got_ref[...], axis=0)
    for k in range(3):
        scores_ref[k, 0] = s[:, k * SLOTS : (k + 1) * SLOTS]
    totals_ref[...] = s[:, 96:99] / s[:, 99:100]


def score_pairs(pos, count, blocks):
    smem = pl.BlockSpec(memory_space=pltpu.SMEM)
    vmem = pl.BlockSpec(memory_space=pltpu.VMEM)
    return pl.pallas_call(
        pair_kernel,
        in_specs=[smem] * 2 + [vmem] * len(blocks),
        out_specs=vmem,
        out_shape=jax.ShapeDtypeStruct((128, 1, L), jnp.float32),
        scratch_shapes=[
            pltpu.VMEM((GROUP, L + 16, D), jnp.bfloat16),
            pltpu.VMEM((GROUP, L, D), jnp.bfloat16),
            pltpu.VMEM((GROUP, 16, L), jnp.bfloat16),
            pltpu.SMEM((4 * SLOTS + GROUP,), jnp.int32),
            pltpu.VMEM((8, L), jnp.int32),
            pltpu.SMEM((8, L), jnp.int32),
            pltpu.SemaphoreType.DMA,
        ],
        compiler_params=pltpu.CompilerParams(vmem_limit_bytes=30 << 20),
        name="score_pairs",
    )(pos, count, *blocks)


def on_device(
    cand_hidden, ref_hidden, cand_ids, ref_ids, cand_len, reference_length, idf_table, up_weight,
    up_bias, down_weight, down_bias, norm_gain, norm_bias, pair_cand, pair_ref, pair_count,
):
    table = jnp.pad(idf_table, (0, TABLE_ROWS * 128 - idf_table.shape[0])).reshape(TABLE_ROWS, 128)
    count = pair_count.reshape(1)
    dp, prompt = lax.axis_index("dp"), lax.axis_index("prompt")
    pos = jnp.stack([dp >> 1, dp & 1, prompt >> 2, prompt & 3]).astype(jnp.int32)
    layer = (
        up_weight,
        up_bias.reshape(1, -1),
        down_weight,
        down_bias.reshape(1, -1),
        norm_gain.reshape(1, -1),
        norm_bias.reshape(1, -1),
    )
    hidden = ref_hidden.reshape(4, L, D)
    words = (
        cand_len.reshape(1),
        reference_length.reshape(4),
        count,
        cand_ids.reshape(1, L),
        ref_ids.reshape(4, L),
        pair_cand.reshape(1, SLOTS),
        pair_ref.reshape(1, SLOTS),
        table,
    )
    cand, refs_a = encode((0, 1, 2), cand_hidden.reshape(1, L, D), hidden, words, layer)
    c1 = send(cand, along_first(1))
    c3 = send(cand, along_first(-1))
    c2 = send(cand, along_first(2))
    back_a = send(refs_a, along_x(1))
    ahead_a = send(refs_a, along_x(-1))
    c1, c2, c3, hidden, pos = lax.optimization_barrier((c1, c2, c3, hidden, pos))
    own4 = jnp.stack([cand, c1, c2, c3])
    d1 = send(own4, along_second(1))
    d2 = send(own4, along_second(-1))
    (refs_b,) = encode((3,), None, hidden, (), layer)
    back_a, ahead_a, refs_b = lax.optimization_barrier((back_a, ahead_a, refs_b))
    back_b = send(refs_b, along_x(1))
    ahead_b = send(refs_b, along_x(-1))
    far_a = send(back_a, along_x(1))
    d3 = send(d1[:2], along_second(1))
    d4 = send(d2[2:], along_second(-1))
    own4, d1, d2 = lax.optimization_barrier((own4, d1, d2))
    others = [send(v, to_other_core) for v in (own4, d1, d2)]
    d3, d4, far_a, back_b, ahead_b = lax.optimization_barrier((d3, d4, far_a, back_b, ahead_b))
    far_b = send(back_b, along_x(1))
    others += [send(v, to_other_core) for v in (d3, d4)]
    cands = [own4, d1, d2, d3, d4, *others]
    blocks = [refs_a, refs_b, back_a, back_b, ahead_a, ahead_b, far_a, far_b]
    payload = score_pairs(pos, count, [*cands, *blocks])
    got = lax.all_to_all(payload, AXES, 0, 0)
    scores, totals = pl.pallas_call(
        finish_kernel,
        out_shape=[
            jax.ShapeDtypeStruct((3, 1, 1, SLOTS), jnp.float32),
            jax.ShapeDtypeStruct((1, 3), jnp.float32),
        ],
        name="finish",
    )(got)
    return scores, totals.reshape(3)


def solution(mesh):
    placed = (
        P("prompt", "dp", None, None),
        P("dp", "prompt", None, None),
        P("prompt", "dp", None),
        P("dp", "prompt", None),
        P("prompt", "dp"),
        P("dp", "prompt"),
        P(),
        P(),
        P(),
        P(),
        P(),
        P(),
        P(),
        P("dp", "prompt", None),
        P("dp", "prompt", None),
        P("dp", "prompt"),
    )
    return jax.shard_map(
        on_device,
        mesh=mesh,
        in_specs=placed,
        out_specs=(P(None, "dp", "prompt", None), P()),
        check_vma=False,
    )
```

```python
import functools

import jax
import jax.numpy as jnp
from jax import lax
from jax.experimental import pallas as pl
from jax.experimental.pallas import tpu as pltpu
from jax.sharding import PartitionSpec as P

D = 1024
L = 128
SLOTS = 32
TABLE_ROWS = 400
AXES = ("dp", "prompt")
GRID = [(y, c, x, z) for y in range(4) for c in range(2) for x in range(4) for z in range(4)]


def number(y, c, x, z):
    return (((y % 4) * 2 + c) * 4 + x % 4) * 4 + z % 4


def send(value, where):
    return lax.ppermute(value, AXES, [(number(*a), number(*where(*a))) for a in GRID])


def along_x(step):
    return lambda y, c, x, z: (y, c, x + (step if c == 0 else -step), z)


def along_first(step):
    return lambda y, c, x, z: (y + step, c, x, z) if c == 0 else (y, c, x, z + step)


def along_second(step):
    return lambda y, c, x, z: (y, c, x, z + step) if c == 0 else (y + step, c, x, z)


def along_z(step):
    return lambda y, c, x, z: (y, c, x, z + step)


def to_other_core(y, c, x, z):
    return (y, 1 - c, x, z)


def encode_kernel(n_cand, picks, weights, sub, *refs):
    refs = list(refs)
    if weights:
        clen_ref, rlen_ref, count_ref, cid_ref, rid_ref, pc_ref, pr_ref, tbl_ref = refs[:8]
        refs = refs[8:]
    ch_ref = refs.pop(0) if n_cand else None
    rh_ref, up, upb, dn, dnb, gain, bias = refs[:7]
    refs = refs[7:]
    co_ref = refs.pop(0) if n_cand else None
    ro_ref, x_ref, acc_ref = refs
    step = pl.program_id(0)
    seqs = n_cand + len(picks)

    @pl.when(step == 0)
    def _():
        if n_cand:
            x_ref[0:L, :] = ch_ref[0]
        for k, q in enumerate(picks):
            x_ref[L * (n_cand + k) : L * (n_cand + k + 1), :] = rh_ref[q]
        if weights:
            ids = jnp.concatenate([cid_ref[...]] + [rid_ref[q : q + 1, :] for q in range(4)], axis=1)
            high, low = ids >> 7, ids & 127
            hot = lax.broadcasted_iota(jnp.int32, (TABLE_ROWS, 5 * L), 0) == high
            rows = lax.dot_general(
                tbl_ref[...].astype(jnp.bfloat16), hot.astype(jnp.bfloat16), (((0,), (0,)), ((), ())),
                preferred_element_type=jnp.float32,
            )
            mine = lax.broadcasted_iota(jnp.int32, (128, 5 * L), 0) == low
            value = jnp.sum(jnp.where(mine, rows, 0.0), axis=0, keepdims=True)
            place = lax.broadcasted_iota(jnp.int32, (1, L), 1)

            def token_weights(k, length):
                return jnp.where(place < length, value[:, k * L : (k + 1) * L], 0.0)

            row = lax.broadcasted_iota(jnp.int32, (16, L), 0)
            co_ref[L:, :] = jnp.zeros((16, D), jnp.bfloat16)
            ro_ref[len(picks) * L :, :] = jnp.zeros((16, D), jnp.bfloat16)
            w = token_weights(0, clen_ref[0])
            count = jnp.full((1, 2 * SLOTS), count_ref[0], jnp.int32)
            slots = jnp.concatenate([pc_ref[...], pr_ref[...], count], axis=1).astype(jnp.float32)
            words = jnp.where(row == 0, w, jnp.where(row == 1, slots, 0.0))
            co_ref[L:, 0:L] = words.astype(jnp.bfloat16)
            block = jnp.zeros((16, L), jnp.float32)
            for q in range(4):
                block = jnp.where(row == q, token_weights(q + 1, rlen_ref[q]), block)
            ro_ref[len(picks) * L :, 0:L] = block.astype(jnp.bfloat16)

    w = up.shape[1] // sub
    x = x_ref[...]
    pre = [
        jnp.dot(x, up[:, k * w : (k + 1) * w], preferred_element_type=jnp.float32)
        + upb[:, k * w : (k + 1) * w]
        for k in range(sub)
    ]
    part = None
    for k in range(sub):
        h = pre[k]
        act = (0.5 * h * (lax.erf(h * 0.7071067811865476) + 1.0)).astype(jnp.bfloat16)
        d = jnp.dot(act, dn[k * w : (k + 1) * w, :], preferred_element_type=jnp.float32)
        part = d if part is None else part + d

    @pl.when(step == 0)
    def _():
        acc_ref[...] = part

    @pl.when(step > 0)
    def _():
        acc_ref[...] += part

    @pl.when(step == pl.num_programs(0) - 1)
    def _():
        for c in range(0, seqs * L, 64):
            r = slice(c, c + 64)
            s = x_ref[r, :].astype(jnp.float32) + acc_ref[r, :] + dnb[...]
            center = jnp.mean(s, axis=-1, keepdims=True)
            e = s - center
            spread = jnp.mean(e * e, axis=-1, keepdims=True)
            y = e * lax.rsqrt(spread + 1e-5) * gain[...] + bias[...]
            m = jnp.sum(y * y, axis=-1, keepdims=True)
            unit = (y * lax.rsqrt(m + 1e-6)).astype(jnp.bfloat16)
            if c < L * n_cand:
                co_ref[r, :] = unit
            else:
                ro_ref[c - L * n_cand : c - L * n_cand + 64, :] = unit


def encode(picks, cand, rh, words, layer, f=1024, sub=4):
    def full(a):
        return pl.BlockSpec(a.shape, lambda i: (0,) * a.ndim, pipeline_mode=pl.Buffered(1))

    up, upb, dn, dnb, gain, bias = layer
    n_cand = 0 if cand is None else 1
    extra = 16 if words else 0
    seqs = n_cand + len(picks)
    smem = pl.BlockSpec(memory_space=pltpu.SMEM)
    outs = [jax.ShapeDtypeStruct((L + extra, D), jnp.bfloat16)] * n_cand + [
        jax.ShapeDtypeStruct((len(picks) * L + extra, D), jnp.bfloat16)
    ]
    first = list(words) + ([cand] if n_cand else []) + [rh]
    return pl.pallas_call(
        functools.partial(encode_kernel, n_cand, picks, bool(words), sub),
        grid=(up.shape[1] // f,),
        in_specs=[smem if k < 3 and words else full(a) for k, a in enumerate(first)]
        + [
            pl.BlockSpec((D, f), lambda i: (0, i)),
            pl.BlockSpec((1, f), lambda i: (0, i)),
            pl.BlockSpec((f, D), lambda i: (i, 0)),
            full(dnb),
            full(gain),
            full(bias),
        ],
        out_specs=[pl.BlockSpec(o.shape, lambda i: (0, 0)) for o in outs],
        out_shape=outs,
        scratch_shapes=[
            pltpu.VMEM((seqs * L, D), jnp.bfloat16),
            pltpu.VMEM((seqs * L, D), jnp.float32),
        ],
        compiler_params=pltpu.CompilerParams(
            dimension_semantics=("arbitrary",), vmem_limit_bytes=60 << 20
        ),
        cost_estimate=pl.CostEstimate(
            flops=4 * seqs * L * D * up.shape[1], bytes_accessed=17 << 20, transcendentals=0
        ),
        name="encode",
    )(*first, up, upb, dn, dnb, gain, bias)


GROUP = 8


def pair_kernel(pos_ref, count_ref, *refs):
    cands, blocks, refs = refs[:9], refs[9:13], refs[13:]
    out_ref, cbuf, rbuf, wbuf, todo, lint, lists, lsem = refs
    y, core, x, z = pos_ref[0], pos_ref[1], pos_ref[2], pos_ref[3]

    lint[...] = jnp.zeros((8, L), jnp.int32)
    for own, places in ((0, ((0, 0), (1, 0), (2, 0), (3, 0))), (1, ((0, 0), (0, 1), (0, 3), (0, 2)))):
        @pl.when(core == own)
        def _(places=places):
            for k, (buf, row) in enumerate(places):
                words = cands[buf][row, L : L + 16, 0:L].astype(jnp.float32)
                lint[k : k + 1, :] = words[1:2, :].astype(jnp.int32)

    lane = lax.broadcasted_iota(jnp.int32, (8, L), 1)
    sub = lax.broadcasted_iota(jnp.int32, (8, L), 0)
    c = lint[...]
    r = pltpu.roll(c, L - SLOTS, 1)
    live = (lane < SLOTS) & (lane < pltpu.roll(c, 2 * SLOTS, 1)) & ((r & 3) == z)
    dz = jnp.where(sub == 1, 3, jnp.where(sub == 2, 1, jnp.where(sub == 3, 2, 0)))
    dx = (((r & 15) >> 2) - x) & 3
    dy = ((c >> 1) - y) & 3
    even = (c & 1) == 0
    u1 = jnp.where(even, dy, dz)
    u2 = jnp.where(even, dz, dy)
    i1 = (4 - u1) & 3
    g2 = jnp.where(u2 == 3, 1, jnp.where(u2 == 1, 2, jnp.where(u2 == 2, jnp.where(i1 >= 2, 4, 3), 0)))
    mine = (c & 1) == core
    source = jnp.where(mine, g2, 5 + jnp.minimum(g2, 3))
    row = jnp.where(mine & (g2 == 4), i1 - 2, i1)
    back = jnp.where(core == 0, 3, 1)
    rs = jnp.where(dx == 0, 0, jnp.where(dx == 2, 3, jnp.where(dx == back, 1, 2)))
    i = (r >> 4) & 3
    code = source | (row << 4) | (rs << 6) | (i << 8) | (((z + dz) & 3) << 10) | (lane << 12)
    lint[...] = jnp.where(live, code, -1)
    move = pltpu.make_async_copy(lint, lists, lsem)
    move.start()
    move.wait()

    def scan(s, n):
        for k in range(4):
            v = lists[k, s]
            todo[n] = v
            n = n + jnp.where(v >= 0, 1, 0)
        return n

    n = lax.fori_loop(0, SLOTS, scan, jnp.int32(0))
    eye = lax.broadcasted_iota(jnp.int32, (L, L), 0) == lax.broadcasted_iota(jnp.int32, (L, L), 1)

    def choose(v, low, high, act):
        if high - low == 1:
            act(low)
            return
        middle = (low + high) // 2

        @pl.when(v < middle)
        def _():
            choose(v, low, middle, act)

        @pl.when(v >= middle)
        def _():
            choose(v, middle, high, act)

    def fetch(t, b):
        code = todo[t]
        row = (code >> 4) & 3
        i = (code >> 8) & 3
        at = pl.multiple_of(i * L, L)

        def take_cand(k):
            cbuf[b] = cands[k][row]

        def take_ref(k):
            rbuf[b] = blocks[k][pl.ds(at, L), :]
            wbuf[b] = blocks[k][4 * L : 4 * L + 16, 0:L]

        choose(code & 15, 0, 9, take_cand)
        choose((code >> 6) & 3, 0, 4, take_ref)

    def one(t, b):
        similar = lax.dot_general(
            cbuf[b, 0:L, :], rbuf[b], (((1,), (1,)), ((), ())), preferred_element_type=jnp.float32
        )
        cw = cbuf[b, L:, 0:L].astype(jnp.float32)[0:1, :]
        wide = wbuf[b].astype(jnp.float32)
        rsub = lax.broadcasted_iota(jnp.int32, (16, L), 0)
        rw = jnp.sum(jnp.where(rsub == ((todo[t] >> 8) & 3), wide, 0.0), axis=0, keepdims=True)
        cw_col = jnp.sum(jnp.where(eye, cw, 0.0), axis=1, keepdims=True)
        row_best = jnp.max(jnp.where(rw > 0, similar, -10000.0), axis=1, keepdims=True)
        col_best = jnp.max(jnp.where(cw_col > 0, similar, -10000.0), axis=0, keepdims=True)
        precision = jnp.sum(cw_col * row_best, axis=0, keepdims=True) / jnp.sum(
            cw, axis=1, keepdims=True
        )
        recall = jnp.sum(rw * col_best, axis=1, keepdims=True) / jnp.sum(rw, axis=1, keepdims=True)
        fmeasure = 2.0 * precision * recall / jnp.maximum(precision + recall, 0.7)
        return precision, recall, fmeasure

    def group(g, carry):
        acc, total = carry
        for k in range(GROUP):
            t = g * GROUP + k

            @pl.when(t < n)
            def _(t=t, k=k):
                fetch(t, k)

        scores = []
        for k in range(GROUP):
            t = g * GROUP + k
            scores.append((t, g * GROUP + k < n, one(t, k)))
        for t, real, (p, r, f) in scores:
            three = jnp.where(lane < 32, p, jnp.where(lane < 64, r, f))
            here = (sub == ((todo[t] >> 10) & 3)) & ((lane & 31) == ((todo[t] >> 12) & 31)) & (lane < 96) & real
            acc = jnp.where(here, three, acc)
            rows = jnp.where(sub == 0, p, jnp.where(sub == 1, r, f))
            total = total + jnp.where(real, rows, 0.0)
        return acc, total

    zero = jnp.zeros((8, L), jnp.float32)
    acc, total = lax.fori_loop(0, (n + GROUP - 1) // GROUP, group, (zero, zero))
    line = lax.broadcasted_iota(jnp.int32, (1, L), 1)
    count = count_ref[0].astype(jnp.float32)
    sums = jnp.where(
        line == 96,
        total[0:1, :],
        jnp.where(line == 97, total[1:2, :], jnp.where(line == 98, total[2:3, :], count)),
    )
    sums = jnp.where((line >= 96) & (line < 100), sums, 0.0)
    out_ref[...] = jnp.broadcast_to(sums[None], out_ref.shape)
    mine = (y * 2 + core) * 4 + x
    for q in range(4):
        out_ref[mine * 4 + q] = acc[q : q + 1, :] + sums


def finish_kernel(got_ref, scores_ref, totals_ref):
    s = jnp.sum(got_ref[...], axis=0)
    for k in range(3):
        scores_ref[k, 0] = s[:, k * SLOTS : (k + 1) * SLOTS]
    totals_ref[...] = s[:, 96:99] / s[:, 99:100]


def pass_on_kernel(pos_ref, out_ref):
    for k in range(4):
        out_ref[k] = pos_ref[k]


def pass_on(pos):
    smem = pl.BlockSpec(memory_space=pltpu.SMEM)
    return pl.pallas_call(
        pass_on_kernel,
        in_specs=[smem],
        out_specs=smem,
        out_shape=jax.ShapeDtypeStruct((4,), jnp.int32),
        cost_estimate=pl.CostEstimate(flops=17250000000, bytes_accessed=1024, transcendentals=0),
        name="pass_on",
    )(pos)


def score_pairs(pos, count, blocks):
    smem = pl.BlockSpec(memory_space=pltpu.SMEM)
    vmem = pl.BlockSpec(memory_space=pltpu.VMEM)
    return pl.pallas_call(
        pair_kernel,
        in_specs=[smem] * 2 + [vmem] * len(blocks),
        out_specs=vmem,
        out_shape=jax.ShapeDtypeStruct((128, 1, L), jnp.float32),
        scratch_shapes=[
            pltpu.VMEM((GROUP, L + 16, D), jnp.bfloat16),
            pltpu.VMEM((GROUP, L, D), jnp.bfloat16),
            pltpu.VMEM((GROUP, 16, L), jnp.bfloat16),
            pltpu.SMEM((4 * SLOTS + GROUP,), jnp.int32),
            pltpu.VMEM((8, L), jnp.int32),
            pltpu.SMEM((8, L), jnp.int32),
            pltpu.SemaphoreType.DMA,
        ],
        compiler_params=pltpu.CompilerParams(vmem_limit_bytes=30 << 20),
        name="score_pairs",
    )(pos, count, *blocks)


def on_device(
    cand_hidden, ref_hidden, cand_ids, ref_ids, cand_len, reference_length, idf_table, up_weight,
    up_bias, down_weight, down_bias, norm_gain, norm_bias, pair_cand, pair_ref, pair_count,
):
    table = jnp.pad(idf_table, (0, TABLE_ROWS * 128 - idf_table.shape[0])).reshape(TABLE_ROWS, 128)
    count = pair_count.reshape(1)
    dp, prompt = lax.axis_index("dp"), lax.axis_index("prompt")
    pos = jnp.stack([dp >> 1, dp & 1, prompt >> 2, prompt & 3]).astype(jnp.int32)
    layer = (
        up_weight,
        up_bias.reshape(1, -1),
        down_weight,
        down_bias.reshape(1, -1),
        norm_gain.reshape(1, -1),
        norm_bias.reshape(1, -1),
    )
    hidden = ref_hidden.reshape(4, L, D)
    words = (
        cand_len.reshape(1),
        reference_length.reshape(4),
        count,
        cand_ids.reshape(1, L),
        ref_ids.reshape(4, L),
        pair_cand.reshape(1, SLOTS),
        pair_ref.reshape(1, SLOTS),
        table,
    )
    cand, refs = encode((0, 1, 2, 3), cand_hidden.reshape(1, L, D), hidden, words, layer)
    back = send(refs, along_x(1))
    ahead = send(refs, along_x(-1))
    back, ahead = lax.optimization_barrier((back, ahead))
    far = send(back, along_x(1))
    c1 = send(cand, along_first(1))
    c3 = send(cand, along_first(-1))
    c2 = send(cand, along_first(2))
    own4 = jnp.stack([cand, c1, c2, c3])
    d1 = send(own4, along_second(1))
    d2 = send(own4, along_second(-1))
    d3 = send(d1[:2], along_second(1))
    d4 = send(d2[2:], along_second(-1))
    own4, d1, d2 = lax.optimization_barrier((own4, d1, d2))
    others = [send(v, to_other_core) for v in (own4, d1, d2)]
    others.append(send(jnp.concatenate([d3, d4]), to_other_core))
    far, pos = lax.optimization_barrier((far, pos))
    pos = pass_on(pos)
    cands = [own4, d1, d2, d3, d4, *others]
    blocks = [refs, back, ahead, far]
    payload = score_pairs(pos, count, [*cands, *blocks])
    got = lax.all_to_all(payload, AXES, 0, 0)
    scores, totals = pl.pallas_call(
        finish_kernel,
        out_shape=[
            jax.ShapeDtypeStruct((3, 1, 1, SLOTS), jnp.float32),
            jax.ShapeDtypeStruct((1, 3), jnp.float32),
        ],
        name="finish",
    )(got)
    return scores, totals.reshape(3)


def solution(mesh):
    placed = (
        P("prompt", "dp", None, None),
        P("dp", "prompt", None, None),
        P("prompt", "dp", None),
        P("dp", "prompt", None),
        P("prompt", "dp"),
        P("dp", "prompt"),
        P(),
        P(),
        P(),
        P(),
        P(),
        P(),
        P(),
        P("dp", "prompt", None),
        P("dp", "prompt", None),
        P("dp", "prompt"),
    )
    return jax.shard_map(
        on_device,
        mesh=mesh,
        in_specs=placed,
        out_specs=(P(None, "dp", "prompt", None), P()),
        check_vma=False,
    )
```

```python
import functools

import jax
import jax.numpy as jnp
from jax import lax
from jax.experimental import pallas as pl
from jax.experimental.pallas import tpu as pltpu
from jax.sharding import PartitionSpec as P

D = 1024
L = 128
SLOTS = 32
TABLE_ROWS = 400
AXES = ("dp", "prompt")
GRID = [(y, c, x, z) for y in range(4) for c in range(2) for x in range(4) for z in range(4)]


def number(y, c, x, z):
    return (((y % 4) * 2 + c) * 4 + x % 4) * 4 + z % 4


def send(value, where):
    return lax.ppermute(value, AXES, [(number(*a), number(*where(*a))) for a in GRID])


def along_x(step):
    return lambda y, c, x, z: (y, c, x + (step if c == 0 else -step), z)


def along_first(step):
    return lambda y, c, x, z: (y + step, c, x, z) if c == 0 else (y, c, x, z + step)


def along_second(step):
    return lambda y, c, x, z: (y, c, x, z + step) if c == 0 else (y + step, c, x, z)


def along_z(step):
    return lambda y, c, x, z: (y, c, x, z + step)


def to_other_core(y, c, x, z):
    return (y, 1 - c, x, z)


def encode_kernel(n_cand, picks, weights, sub, *refs):
    refs = list(refs)
    if weights:
        clen_ref, rlen_ref, count_ref, cid_ref, rid_ref, pc_ref, pr_ref, tbl_ref = refs[:8]
        refs = refs[8:]
    ch_ref = refs.pop(0) if n_cand else None
    rh_ref, up, upb, dn, dnb, gain, bias = refs[:7]
    refs = refs[7:]
    co_ref = refs.pop(0) if n_cand else None
    ro_ref, x_ref, acc_ref = refs
    step = pl.program_id(0)
    seqs = n_cand + len(picks)

    def token_weights(ids, length):
        high, low = ids >> 7, ids & 127
        hot = (lax.broadcasted_iota(jnp.int32, (TABLE_ROWS, L), 0) == high).astype(jnp.bfloat16)
        rows = lax.dot_general(
            tbl_ref[...].astype(jnp.bfloat16), hot, (((0,), (0,)), ((), ())), preferred_element_type=jnp.float32
        )
        mine = lax.broadcasted_iota(jnp.int32, (128, L), 0) == low
        value = jnp.sum(jnp.where(mine, rows, 0.0), axis=0, keepdims=True)
        live = lax.broadcasted_iota(jnp.int32, (1, L), 1) < length
        return jnp.where(live, value, 0.0)

    @pl.when(step == 0)
    def _():
        if n_cand:
            x_ref[0:L, :] = ch_ref[0]
        for k, q in enumerate(picks):
            x_ref[L * (n_cand + k) : L * (n_cand + k + 1), :] = rh_ref[q]
        if weights:
            row = lax.broadcasted_iota(jnp.int32, (16, L), 0)
            co_ref[L:, :] = jnp.zeros((16, D), jnp.bfloat16)
            ro_ref[len(picks) * L :, :] = jnp.zeros((16, D), jnp.bfloat16)
            w = token_weights(cid_ref[...], clen_ref[0])
            count = jnp.full((1, 2 * SLOTS), count_ref[0], jnp.int32)
            slots = jnp.concatenate([pc_ref[...], pr_ref[...], count], axis=1).astype(jnp.float32)
            words = jnp.where(row == 0, w, jnp.where(row == 1, slots, 0.0))
            co_ref[L:, 0:L] = words.astype(jnp.bfloat16)
            block = jnp.zeros((16, L), jnp.float32)
            for q in range(4):
                block = jnp.where(row == q, token_weights(rid_ref[q : q + 1, :], rlen_ref[q]), block)
            ro_ref[len(picks) * L :, 0:L] = block.astype(jnp.bfloat16)

    w = up.shape[1] // sub
    x = x_ref[...]
    pre = [
        jnp.dot(x, up[:, k * w : (k + 1) * w], preferred_element_type=jnp.float32)
        + upb[:, k * w : (k + 1) * w]
        for k in range(sub)
    ]
    part = None
    for k in range(sub):
        h = pre[k]
        act = (0.5 * h * (lax.erf(h * 0.7071067811865476) + 1.0)).astype(jnp.bfloat16)
        d = jnp.dot(act, dn[k * w : (k + 1) * w, :], preferred_element_type=jnp.float32)
        part = d if part is None else part + d

    @pl.when(step == 0)
    def _():
        acc_ref[...] = part

    @pl.when(step > 0)
    def _():
        acc_ref[...] += part

    @pl.when(step == pl.num_programs(0) - 1)
    def _():
        for c in range(0, seqs * L, 64):
            r = slice(c, c + 64)
            s = x_ref[r, :].astype(jnp.float32) + acc_ref[r, :] + dnb[...]
            center = jnp.mean(s, axis=-1, keepdims=True)
            e = s - center
            spread = jnp.mean(e * e, axis=-1, keepdims=True)
            y = e * lax.rsqrt(spread + 1e-5) * gain[...] + bias[...]
            m = jnp.sum(y * y, axis=-1, keepdims=True)
            unit = (y * lax.rsqrt(m + 1e-6)).astype(jnp.bfloat16)
            if c < L * n_cand:
                co_ref[r, :] = unit
            else:
                ro_ref[c - L * n_cand : c - L * n_cand + 64, :] = unit


def encode(picks, cand, rh, words, layer, f=1024, sub=4):
    def full(a):
        return pl.BlockSpec(a.shape, lambda i: (0,) * a.ndim, pipeline_mode=pl.Buffered(1))

    up, upb, dn, dnb, gain, bias = layer
    n_cand = 0 if cand is None else 1
    extra = 16 if words else 0
    seqs = n_cand + len(picks)
    smem = pl.BlockSpec(memory_space=pltpu.SMEM)
    outs = [jax.ShapeDtypeStruct((L + extra, D), jnp.bfloat16)] * n_cand + [
        jax.ShapeDtypeStruct((len(picks) * L + extra, D), jnp.bfloat16)
    ]
    first = list(words) + ([cand] if n_cand else []) + [rh]
    return pl.pallas_call(
        functools.partial(encode_kernel, n_cand, picks, bool(words), sub),
        grid=(up.shape[1] // f,),
        in_specs=[smem if k < 3 and words else full(a) for k, a in enumerate(first)]
        + [
            pl.BlockSpec((D, f), lambda i: (0, i)),
            pl.BlockSpec((1, f), lambda i: (0, i)),
            pl.BlockSpec((f, D), lambda i: (i, 0)),
            full(dnb),
            full(gain),
            full(bias),
        ],
        out_specs=[pl.BlockSpec(o.shape, lambda i: (0, 0)) for o in outs],
        out_shape=outs,
        scratch_shapes=[
            pltpu.VMEM((seqs * L, D), jnp.bfloat16),
            pltpu.VMEM((seqs * L, D), jnp.float32),
        ],
        compiler_params=pltpu.CompilerParams(
            dimension_semantics=("arbitrary",), vmem_limit_bytes=60 << 20
        ),
        cost_estimate=pl.CostEstimate(
            flops=4 * seqs * L * D * up.shape[1], bytes_accessed=17 << 20, transcendentals=0
        ),
        name="encode",
    )(*first, up, upb, dn, dnb, gain, bias)


GROUP = 8
AHEAD = 3


def pair_kernel(pos_ref, count_ref, *refs):
    cands, blocks, refs = refs[:10], refs[10:18], refs[18:]
    out_ref, cbuf, rbuf, wbuf, todo, lint, lists, lsem = refs
    y, core, x, z = pos_ref[0], pos_ref[1], pos_ref[2], pos_ref[3]

    lint[...] = jnp.zeros((8, L), jnp.int32)
    for own, places in ((0, ((0, 0), (1, 0), (2, 0), (3, 0))), (1, ((0, 0), (0, 1), (0, 3), (0, 2)))):
        @pl.when(core == own)
        def _(places=places):
            for k, (buf, row) in enumerate(places):
                words = cands[buf][row, L : L + 16, 0:L].astype(jnp.float32)
                lint[k : k + 1, :] = words[1:2, :].astype(jnp.int32)

    lane = lax.broadcasted_iota(jnp.int32, (8, L), 1)
    sub = lax.broadcasted_iota(jnp.int32, (8, L), 0)
    c = lint[...]
    r = pltpu.roll(c, L - SLOTS, 1)
    live = (lane < SLOTS) & (lane < pltpu.roll(c, 2 * SLOTS, 1)) & ((r & 3) == z)
    dz = jnp.where(sub == 1, 3, jnp.where(sub == 2, 1, jnp.where(sub == 3, 2, 0)))
    dx = (((r & 15) >> 2) - x) & 3
    dy = ((c >> 1) - y) & 3
    even = (c & 1) == 0
    u1 = jnp.where(even, dy, dz)
    u2 = jnp.where(even, dz, dy)
    i1 = (4 - u1) & 3
    g2 = jnp.where(u2 == 3, 1, jnp.where(u2 == 1, 2, jnp.where(u2 == 2, jnp.where(i1 >= 2, 4, 3), 0)))
    source = g2 + jnp.where((c & 1) == core, 0, 5)
    row = jnp.where(g2 == 4, i1 - 2, i1)
    back = jnp.where(core == 0, 3, 1)
    rs = jnp.where(dx == 0, 0, jnp.where(dx == 2, 3, jnp.where(dx == back, 1, 2)))
    i = (r >> 4) & 3
    code = source | (row << 4) | (rs << 6) | (i << 8) | (((z + dz) & 3) << 10) | (lane << 12)
    lint[...] = jnp.where(live, code, -1)
    move = pltpu.make_async_copy(lint, lists, lsem)
    move.start()
    move.wait()

    def scan(s, n):
        for k in range(4):
            v = lists[k, s]
            todo[n] = v
            n = n + jnp.where(v >= 0, 1, 0)
        return n

    n = lax.fori_loop(0, SLOTS, scan, jnp.int32(0))
    eye = lax.broadcasted_iota(jnp.int32, (L, L), 0) == lax.broadcasted_iota(jnp.int32, (L, L), 1)

    def choose(v, low, high, act):
        if high - low == 1:
            act(low)
            return
        middle = (low + high) // 2

        @pl.when(v < middle)
        def _():
            choose(v, low, middle, act)

        @pl.when(v >= middle)
        def _():
            choose(v, middle, high, act)

    def fetch(t, b):
        code = todo[t]
        row = (code >> 4) & 3
        i = (code >> 8) & 3
        at = pl.multiple_of(jnp.where(i < AHEAD, i, i - AHEAD) * L, L)

        def take_cand(k):
            cbuf[b] = cands[k][row]

        def take_ref(k):
            rbuf[b] = blocks[k][pl.ds(at, L), :]
            wbuf[b] = blocks[k - k % 2][AHEAD * L : AHEAD * L + 16, 0:L]

        choose(code & 15, 0, 10, take_cand)
        choose(((code >> 6) & 3) * 2 + jnp.where(i < AHEAD, 0, 1), 0, 8, take_ref)

    def one(t, b):
        similar = lax.dot_general(
            cbuf[b, 0:L, :], rbuf[b], (((1,), (1,)), ((), ())), preferred_element_type=jnp.float32
        )
        cw = cbuf[b, L:, 0:L].astype(jnp.float32)[0:1, :]
        wide = wbuf[b].astype(jnp.float32)
        rsub = lax.broadcasted_iota(jnp.int32, (16, L), 0)
        rw = jnp.sum(jnp.where(rsub == ((todo[t] >> 8) & 3), wide, 0.0), axis=0, keepdims=True)
        cw_col = jnp.sum(jnp.where(eye, cw, 0.0), axis=1, keepdims=True)
        row_best = jnp.max(jnp.where(rw > 0, similar, -10000.0), axis=1, keepdims=True)
        col_best = jnp.max(jnp.where(cw_col > 0, similar, -10000.0), axis=0, keepdims=True)
        precision = jnp.sum(cw_col * row_best, axis=0, keepdims=True) / jnp.sum(
            cw, axis=1, keepdims=True
        )
        recall = jnp.sum(rw * col_best, axis=1, keepdims=True) / jnp.sum(rw, axis=1, keepdims=True)
        fmeasure = 2.0 * precision * recall / jnp.maximum(precision + recall, 0.7)
        return precision, recall, fmeasure

    def group(g, carry):
        acc, total = carry
        for k in range(GROUP):
            t = g * GROUP + k

            @pl.when(t < n)
            def _(t=t, k=k):
                fetch(t, k)

        scores = []
        for k in range(GROUP):
            t = g * GROUP + k
            scores.append((t, g * GROUP + k < n, one(t, k)))
        for t, real, (p, r, f) in scores:
            three = jnp.where(lane < 32, p, jnp.where(lane < 64, r, f))
            here = (sub == ((todo[t] >> 10) & 3)) & ((lane & 31) == ((todo[t] >> 12) & 31)) & (lane < 96) & real
            acc = jnp.where(here, three, acc)
            rows = jnp.where(sub == 0, p, jnp.where(sub == 1, r, f))
            total = total + jnp.where(real, rows, 0.0)
        return acc, total

    zero = jnp.zeros((8, L), jnp.float32)
    acc, total = lax.fori_loop(0, (n + GROUP - 1) // GROUP, group, (zero, zero))
    line = lax.broadcasted_iota(jnp.int32, (1, L), 1)
    count = count_ref[0].astype(jnp.float32)
    sums = jnp.where(
        line == 96,
        total[0:1, :],
        jnp.where(line == 97, total[1:2, :], jnp.where(line == 98, total[2:3, :], count)),
    )
    sums = jnp.where((line >= 96) & (line < 100), sums, 0.0)
    out_ref[...] = jnp.broadcast_to(sums[None], out_ref.shape)
    mine = (y * 2 + core) * 4 + x
    for q in range(4):
        out_ref[mine * 4 + q] = acc[q : q + 1, :] + sums


def finish_kernel(got_ref, scores_ref, totals_ref):
    s = jnp.sum(got_ref[...], axis=0)
    for k in range(3):
        scores_ref[k, 0] = s[:, k * SLOTS : (k + 1) * SLOTS]
    totals_ref[...] = s[:, 96:99] / s[:, 99:100]


def score_pairs(pos, count, blocks):
    smem = pl.BlockSpec(memory_space=pltpu.SMEM)
    vmem = pl.BlockSpec(memory_space=pltpu.VMEM)
    return pl.pallas_call(
        pair_kernel,
        in_specs=[smem] * 2 + [vmem] * len(blocks),
        out_specs=vmem,
        out_shape=jax.ShapeDtypeStruct((128, 1, L), jnp.float32),
        scratch_shapes=[
            pltpu.VMEM((GROUP, L + 16, D), jnp.bfloat16),
            pltpu.VMEM((GROUP, L, D), jnp.bfloat16),
            pltpu.VMEM((GROUP, 16, L), jnp.bfloat16),
            pltpu.SMEM((4 * SLOTS + GROUP,), jnp.int32),
            pltpu.VMEM((8, L), jnp.int32),
            pltpu.SMEM((8, L), jnp.int32),
            pltpu.SemaphoreType.DMA,
        ],
        compiler_params=pltpu.CompilerParams(vmem_limit_bytes=30 << 20),
        name="score_pairs",
    )(pos, count, *blocks)


def on_device(
    cand_hidden, ref_hidden, cand_ids, ref_ids, cand_len, reference_length, idf_table, up_weight,
    up_bias, down_weight, down_bias, norm_gain, norm_bias, pair_cand, pair_ref, pair_count,
):
    table = jnp.pad(idf_table, (0, TABLE_ROWS * 128 - idf_table.shape[0])).reshape(TABLE_ROWS, 128)
    count = pair_count.reshape(1)
    dp, prompt = lax.axis_index("dp"), lax.axis_index("prompt")
    pos = jnp.stack([dp >> 1, dp & 1, prompt >> 2, prompt & 3]).astype(jnp.int32)
    layer = (
        up_weight,
        up_bias.reshape(1, -1),
        down_weight,
        down_bias.reshape(1, -1),
        norm_gain.reshape(1, -1),
        norm_bias.reshape(1, -1),
    )
    hidden = ref_hidden.reshape(4, L, D)
    words = (
        cand_len.reshape(1),
        reference_length.reshape(4),
        count,
        cand_ids.reshape(1, L),
        ref_ids.reshape(4, L),
        pair_cand.reshape(1, SLOTS),
        pair_ref.reshape(1, SLOTS),
        table,
    )
    cand, refs_a = encode((0, 1, 2), cand_hidden.reshape(1, L, D), hidden, words, layer)
    c1 = send(cand, along_first(1))
    c3 = send(cand, along_first(-1))
    c2 = send(cand, along_first(2))
    back_a = send(refs_a, along_x(1))
    ahead_a = send(refs_a, along_x(-1))
    (refs_b,) = encode((3,), None, hidden, (), layer)
    c1, c2, c3, refs_b, pos = lax.optimization_barrier((c1, c2, c3, refs_b, pos))
    own4 = jnp.stack([cand, c1, c2, c3])
    d1 = send(own4, along_second(1))
    d2 = send(own4, along_second(-1))
    back_b = send(refs_b, along_x(1))
    ahead_b = send(refs_b, along_x(-1))
    back_a, ahead_a, back_b, ahead_b = lax.optimization_barrier((back_a, ahead_a, back_b, ahead_b))
    far_a = send(back_a, along_x(1))
    far_b = send(back_b, along_x(1))
    d3 = send(d1[:2], along_second(1))
    d4 = send(d2[2:], along_second(-1))
    own4, d1, d2 = lax.optimization_barrier((own4, d1, d2))
    others = [send(v, to_other_core) for v in (own4, d1, d2)]
    d3, d4, far_a, far_b = lax.optimization_barrier((d3, d4, far_a, far_b))
    others += [send(v, to_other_core) for v in (d3, d4)]
    cands = [own4, d1, d2, d3, d4, *others]
    blocks = [refs_a, refs_b, back_a, back_b, ahead_a, ahead_b, far_a, far_b]
    payload = score_pairs(pos, count, [*cands, *blocks])
    got = lax.all_to_all(payload, AXES, 0, 0)
    scores, totals = pl.pallas_call(
        finish_kernel,
        out_shape=[
            jax.ShapeDtypeStruct((3, 1, 1, SLOTS), jnp.float32),
            jax.ShapeDtypeStruct((1, 3), jnp.float32),
        ],
        name="finish",
    )(got)
    return scores, totals.reshape(3)


def solution(mesh):
    placed = (
        P("prompt", "dp", None, None),
        P("dp", "prompt", None, None),
        P("prompt", "dp", None),
        P("dp", "prompt", None),
        P("prompt", "dp"),
        P("dp", "prompt"),
        P(),
        P(),
        P(),
        P(),
        P(),
        P(),
        P(),
        P("dp", "prompt", None),
        P("dp", "prompt", None),
        P("dp", "prompt"),
    )
    return jax.shard_map(
        on_device,
        mesh=mesh,
        in_specs=placed,
        out_specs=(P(None, "dp", "prompt", None), P()),
        check_vma=False,
    )
```

```python
import functools

import jax
import jax.numpy as jnp
from jax import lax
from jax.experimental import pallas as pl
from jax.experimental.pallas import tpu as pltpu
from jax.sharding import PartitionSpec as P

D = 1024
L = 128
SLOTS = 32
TABLE_ROWS = 400
AXES = ("dp", "prompt")
GRID = [(y, c, x, z) for y in range(4) for c in range(2) for x in range(4) for z in range(4)]


def number(y, c, x, z):
    return (((y % 4) * 2 + c) * 4 + x % 4) * 4 + z % 4


def send(value, where):
    return lax.ppermute(value, AXES, [(number(*a), number(*where(*a))) for a in GRID])


def along_x(step):
    return lambda y, c, x, z: (y, c, x + (step if c == 0 else -step), z)


def along_first(step):
    return lambda y, c, x, z: (y + step, c, x, z) if c == 0 else (y, c, x, z + step)


def along_second(step):
    return lambda y, c, x, z: (y, c, x, z + step) if c == 0 else (y + step, c, x, z)


def along_z(step):
    return lambda y, c, x, z: (y, c, x, z + step)


def to_other_core(y, c, x, z):
    return (y, 1 - c, x, z)


def encode_kernel(n_cand, picks, weights, sub, *refs):
    refs = list(refs)
    if weights:
        clen_ref, rlen_ref, count_ref, cid_ref, rid_ref, pc_ref, pr_ref, tbl_ref = refs[:8]
        refs = refs[8:]
    ch_ref = refs.pop(0) if n_cand else None
    rh_ref, up, upb, dn, dnb, gain, bias = refs[:7]
    refs = refs[7:]
    co_ref = refs.pop(0) if n_cand else None
    ro_ref, x_ref, acc_ref = refs
    step = pl.program_id(0)
    seqs = n_cand + len(picks)

    @pl.when(step == 0)
    def _():
        if n_cand:
            x_ref[0:L, :] = ch_ref[0]
        for k, q in enumerate(picks):
            x_ref[L * (n_cand + k) : L * (n_cand + k + 1), :] = rh_ref[q]
        if weights:
            full = tbl_ref.shape[0] // 1024
            rest = tbl_ref.shape[0] - full * 1024
            pieces = [tbl_ref[pl.ds(k * 1024, 1024)].reshape(8, 128) for k in range(full)]
            end = jnp.concatenate([tbl_ref[pl.ds(full * 1024, rest)], jnp.zeros((1024 - rest,), jnp.float32)])
            table = jnp.concatenate(pieces + [end.reshape(8, 128)], axis=0).astype(jnp.bfloat16)
            ids = jnp.concatenate([cid_ref[...]] + [rid_ref[q : q + 1, :] for q in range(4)], axis=1)
            high, low = ids >> 7, ids & 127
            hot = lax.broadcasted_iota(jnp.int32, (TABLE_ROWS, 5 * L), 0) == high
            rows = lax.dot_general(
                table, hot.astype(jnp.bfloat16), (((0,), (0,)), ((), ())),
                preferred_element_type=jnp.float32,
            )
            mine = lax.broadcasted_iota(jnp.int32, (128, 5 * L), 0) == low
            value = jnp.sum(jnp.where(mine, rows, 0.0), axis=0, keepdims=True)
            place = lax.broadcasted_iota(jnp.int32, (1, L), 1)

            def token_weights(k, length):
                return jnp.where(place < length, value[:, k * L : (k + 1) * L], 0.0)

            row = lax.broadcasted_iota(jnp.int32, (16, L), 0)
            co_ref[L:, :] = jnp.zeros((16, D), jnp.bfloat16)
            ro_ref[len(picks) * L :, :] = jnp.zeros((16, D), jnp.bfloat16)
            w = token_weights(0, clen_ref[0])
            count = jnp.full((1, 2 * SLOTS), count_ref[0], jnp.int32)
            slots = jnp.concatenate([pc_ref[...], pr_ref[...], count], axis=1).astype(jnp.float32)
            words = jnp.where(row == 0, w, jnp.where(row == 1, slots, 0.0))
            co_ref[L:, 0:L] = words.astype(jnp.bfloat16)
            block = jnp.zeros((16, L), jnp.float32)
            for q in range(4):
                block = jnp.where(row == q, token_weights(q + 1, rlen_ref[q]), block)
            ro_ref[len(picks) * L :, 0:L] = block.astype(jnp.bfloat16)

    w = up.shape[1] // sub
    x = x_ref[...]
    pre = [
        jnp.dot(x, up[:, k * w : (k + 1) * w], preferred_element_type=jnp.float32)
        + upb[:, k * w : (k + 1) * w]
        for k in range(sub)
    ]
    part = None
    for k in range(sub):
        h = pre[k]
        act = (0.5 * h * (lax.erf(h * 0.7071067811865476) + 1.0)).astype(jnp.bfloat16)
        d = jnp.dot(act, dn[k * w : (k + 1) * w, :], preferred_element_type=jnp.float32)
        part = d if part is None else part + d

    @pl.when(step == 0)
    def _():
        acc_ref[...] = part

    @pl.when(step > 0)
    def _():
        acc_ref[...] += part

    @pl.when(step == pl.num_programs(0) - 1)
    def _():
        for c in range(0, seqs * L, 64):
            r = slice(c, c + 64)
            s = x_ref[r, :].astype(jnp.float32) + acc_ref[r, :] + dnb[...]
            center = jnp.mean(s, axis=-1, keepdims=True)
            e = s - center
            spread = jnp.mean(e * e, axis=-1, keepdims=True)
            y = e * lax.rsqrt(spread + 1e-5) * gain[...] + bias[...]
            m = jnp.sum(y * y, axis=-1, keepdims=True)
            unit = (y * lax.rsqrt(m + 1e-6)).astype(jnp.bfloat16)
            if c < L * n_cand:
                co_ref[r, :] = unit
            else:
                ro_ref[c - L * n_cand : c - L * n_cand + 64, :] = unit


def encode(picks, cand, rh, words, layer, f=1024, sub=4):
    def full(a):
        return pl.BlockSpec(a.shape, lambda i: (0,) * a.ndim, pipeline_mode=pl.Buffered(1))

    up, upb, dn, dnb, gain, bias = layer
    n_cand = 0 if cand is None else 1
    extra = 16 if words else 0
    seqs = n_cand + len(picks)
    smem = pl.BlockSpec(memory_space=pltpu.SMEM)
    outs = [jax.ShapeDtypeStruct((L + extra, D), jnp.bfloat16)] * n_cand + [
        jax.ShapeDtypeStruct((len(picks) * L + extra, D), jnp.bfloat16)
    ]
    first = list(words) + ([cand] if n_cand else []) + [rh]
    return pl.pallas_call(
        functools.partial(encode_kernel, n_cand, picks, bool(words), sub),
        grid=(up.shape[1] // f,),
        in_specs=[smem if k < 3 and words else full(a) for k, a in enumerate(first)]
        + [
            pl.BlockSpec((D, f), lambda i: (0, i)),
            pl.BlockSpec((1, f), lambda i: (0, i)),
            pl.BlockSpec((f, D), lambda i: (i, 0)),
            full(dnb),
            full(gain),
            full(bias),
        ],
        out_specs=[pl.BlockSpec(o.shape, lambda i: (0, 0)) for o in outs],
        out_shape=outs,
        scratch_shapes=[
            pltpu.VMEM((seqs * L, D), jnp.bfloat16),
            pltpu.VMEM((seqs * L, D), jnp.float32),
        ],
        compiler_params=pltpu.CompilerParams(
            dimension_semantics=("arbitrary",), vmem_limit_bytes=60 << 20
        ),
        cost_estimate=pl.CostEstimate(
            flops=4 * seqs * L * D * up.shape[1], bytes_accessed=17 << 20, transcendentals=0
        ),
        name="encode",
    )(*first, up, upb, dn, dnb, gain, bias)


GROUP = 8
AHEAD = 3


def pair_kernel(pos_ref, count_ref, *refs):
    cands, blocks, refs = refs[:10], refs[10:18], refs[18:]
    out_ref, cbuf, rbuf, wbuf, todo, lint, lists, lsem = refs
    y, core, x, z = pos_ref[0], pos_ref[1], pos_ref[2], pos_ref[3]

    lint[...] = jnp.zeros((8, L), jnp.int32)
    for own, places in ((0, ((0, 0), (1, 0), (2, 0), (3, 0))), (1, ((0, 0), (0, 1), (0, 3), (0, 2)))):
        @pl.when(core == own)
        def _(places=places):
            for k, (buf, row) in enumerate(places):
                words = cands[buf][row, L : L + 16, 0:L].astype(jnp.float32)
                lint[k : k + 1, :] = words[1:2, :].astype(jnp.int32)

    lane = lax.broadcasted_iota(jnp.int32, (8, L), 1)
    sub = lax.broadcasted_iota(jnp.int32, (8, L), 0)
    c = lint[...]
    r = pltpu.roll(c, L - SLOTS, 1)
    live = (lane < SLOTS) & (lane < pltpu.roll(c, 2 * SLOTS, 1)) & ((r & 3) == z)
    dz = jnp.where(sub == 1, 3, jnp.where(sub == 2, 1, jnp.where(sub == 3, 2, 0)))
    dx = (((r & 15) >> 2) - x) & 3
    dy = ((c >> 1) - y) & 3
    even = (c & 1) == 0
    u1 = jnp.where(even, dy, dz)
    u2 = jnp.where(even, dz, dy)
    i1 = (4 - u1) & 3
    g2 = jnp.where(u2 == 3, 1, jnp.where(u2 == 1, 2, jnp.where(u2 == 2, jnp.where(i1 >= 2, 4, 3), 0)))
    source = g2 + jnp.where((c & 1) == core, 0, 5)
    row = jnp.where(g2 == 4, i1 - 2, i1)
    back = jnp.where(core == 0, 3, 1)
    rs = jnp.where(dx == 0, 0, jnp.where(dx == 2, 3, jnp.where(dx == back, 1, 2)))
    i = (r >> 4) & 3
    code = source | (row << 4) | (rs << 6) | (i << 8) | (((z + dz) & 3) << 10) | (lane << 12)
    lint[...] = jnp.where(live, code, -1)
    move = pltpu.make_async_copy(lint, lists, lsem)
    move.start()
    move.wait()

    def scan(s, n):
        for k in range(4):
            v = lists[k, s]
            todo[n] = v
            n = n + jnp.where(v >= 0, 1, 0)
        return n

    n = lax.fori_loop(0, SLOTS, scan, jnp.int32(0))
    eye = lax.broadcasted_iota(jnp.int32, (L, L), 0) == lax.broadcasted_iota(jnp.int32, (L, L), 1)

    def choose(v, low, high, act):
        if high - low == 1:
            act(low)
            return
        middle = (low + high) // 2

        @pl.when(v < middle)
        def _():
            choose(v, low, middle, act)

        @pl.when(v >= middle)
        def _():
            choose(v, middle, high, act)

    def fetch(t, b):
        code = todo[t]
        row = (code >> 4) & 3
        i = (code >> 8) & 3
        at = pl.multiple_of(jnp.where(i < AHEAD, i, i - AHEAD) * L, L)

        def take_cand(k):
            cbuf[b] = cands[k][row]

        def take_ref(k):
            rbuf[b] = blocks[k][pl.ds(at, L), :]
            wbuf[b] = blocks[k - k % 2][AHEAD * L : AHEAD * L + 16, 0:L]

        choose(code & 15, 0, 10, take_cand)
        choose(((code >> 6) & 3) * 2 + jnp.where(i < AHEAD, 0, 1), 0, 8, take_ref)

    def one(t, b):
        similar = lax.dot_general(
            cbuf[b, 0:L, :], rbuf[b], (((1,), (1,)), ((), ())), preferred_element_type=jnp.float32
        )
        cw = cbuf[b, L:, 0:L].astype(jnp.float32)[0:1, :]
        wide = wbuf[b].astype(jnp.float32)
        rsub = lax.broadcasted_iota(jnp.int32, (16, L), 0)
        rw = jnp.sum(jnp.where(rsub == ((todo[t] >> 8) & 3), wide, 0.0), axis=0, keepdims=True)
        cw_col = jnp.sum(jnp.where(eye, cw, 0.0), axis=1, keepdims=True)
        row_best = jnp.max(jnp.where(rw > 0, similar, -10000.0), axis=1, keepdims=True)
        col_best = jnp.max(jnp.where(cw_col > 0, similar, -10000.0), axis=0, keepdims=True)
        precision = jnp.sum(cw_col * row_best, axis=0, keepdims=True) / jnp.sum(
            cw, axis=1, keepdims=True
        )
        recall = jnp.sum(rw * col_best, axis=1, keepdims=True) / jnp.sum(rw, axis=1, keepdims=True)
        fmeasure = 2.0 * precision * recall / jnp.maximum(precision + recall, 0.7)
        return precision, recall, fmeasure

    def group(g, carry):
        acc, total = carry
        for k in range(GROUP):
            t = g * GROUP + k

            @pl.when(t < n)
            def _(t=t, k=k):
                fetch(t, k)

        scores = []
        for k in range(GROUP):
            t = g * GROUP + k
            scores.append((t, g * GROUP + k < n, one(t, k)))
        for t, real, (p, r, f) in scores:
            three = jnp.where(lane < 32, p, jnp.where(lane < 64, r, f))
            here = (sub == ((todo[t] >> 10) & 3)) & ((lane & 31) == ((todo[t] >> 12) & 31)) & (lane < 96) & real
            acc = jnp.where(here, three, acc)
            rows = jnp.where(sub == 0, p, jnp.where(sub == 1, r, f))
            total = total + jnp.where(real, rows, 0.0)
        return acc, total

    zero = jnp.zeros((8, L), jnp.float32)
    acc, total = lax.fori_loop(0, (n + GROUP - 1) // GROUP, group, (zero, zero))
    line = lax.broadcasted_iota(jnp.int32, (1, L), 1)
    count = count_ref[0].astype(jnp.float32)
    sums = jnp.where(
        line == 96,
        total[0:1, :],
        jnp.where(line == 97, total[1:2, :], jnp.where(line == 98, total[2:3, :], count)),
    )
    sums = jnp.where((line >= 96) & (line < 100), sums, 0.0)
    out_ref[...] = jnp.broadcast_to(sums[None], out_ref.shape)
    mine = (y * 2 + core) * 4 + x
    for q in range(4):
        out_ref[mine * 4 + q] = acc[q : q + 1, :] + sums


def finish_kernel(got_ref, scores_ref, totals_ref):
    s = jnp.sum(got_ref[...], axis=0)
    for k in range(3):
        scores_ref[k, 0] = s[:, k * SLOTS : (k + 1) * SLOTS]
    totals_ref[...] = s[:, 96:99] / s[:, 99:100]


def score_pairs(pos, count, blocks):
    smem = pl.BlockSpec(memory_space=pltpu.SMEM)
    vmem = pl.BlockSpec(memory_space=pltpu.VMEM)
    return pl.pallas_call(
        pair_kernel,
        in_specs=[smem] * 2 + [vmem] * len(blocks),
        out_specs=vmem,
        out_shape=jax.ShapeDtypeStruct((128, 1, L), jnp.float32),
        scratch_shapes=[
            pltpu.VMEM((GROUP, L + 16, D), jnp.bfloat16),
            pltpu.VMEM((GROUP, L, D), jnp.bfloat16),
            pltpu.VMEM((GROUP, 16, L), jnp.bfloat16),
            pltpu.SMEM((4 * SLOTS + GROUP,), jnp.int32),
            pltpu.VMEM((8, L), jnp.int32),
            pltpu.SMEM((8, L), jnp.int32),
            pltpu.SemaphoreType.DMA,
        ],
        compiler_params=pltpu.CompilerParams(vmem_limit_bytes=30 << 20),
        name="score_pairs",
    )(pos, count, *blocks)


def on_device(
    cand_hidden, ref_hidden, cand_ids, ref_ids, cand_len, reference_length, idf_table, up_weight,
    up_bias, down_weight, down_bias, norm_gain, norm_bias, pair_cand, pair_ref, pair_count,
):
    count = pair_count.reshape(1)
    dp, prompt = lax.axis_index("dp"), lax.axis_index("prompt")
    pos = jnp.stack([dp >> 1, dp & 1, prompt >> 2, prompt & 3]).astype(jnp.int32)
    layer = (
        up_weight,
        up_bias.reshape(1, -1),
        down_weight,
        down_bias.reshape(1, -1),
        norm_gain.reshape(1, -1),
        norm_bias.reshape(1, -1),
    )
    hidden = ref_hidden.reshape(4, L, D)
    words = (
        cand_len.reshape(1),
        reference_length.reshape(4),
        count,
        cand_ids.reshape(1, L),
        ref_ids.reshape(4, L),
        pair_cand.reshape(1, SLOTS),
        pair_ref.reshape(1, SLOTS),
        idf_table,
    )
    cand, refs_a = encode((0, 1, 2), cand_hidden.reshape(1, L, D), hidden, words, layer)
    c1 = send(cand, along_first(1))
    c3 = send(cand, along_first(-1))
    c2 = send(cand, along_first(2))
    back_a = send(refs_a, along_x(1))
    ahead_a = send(refs_a, along_x(-1))
    c1, c2, c3, hidden, pos = lax.optimization_barrier((c1, c2, c3, hidden, pos))
    own4 = jnp.stack([cand, c1, c2, c3])
    d1 = send(own4, along_second(1))
    d2 = send(own4, along_second(-1))
    (refs_b,) = encode((3,), None, hidden, (), layer)
    back_a, ahead_a, refs_b = lax.optimization_barrier((back_a, ahead_a, refs_b))
    back_b = send(refs_b, along_x(1))
    ahead_b = send(refs_b, along_x(-1))
    far_a = send(back_a, along_x(1))
    d3 = send(d1[:2], along_second(1))
    d4 = send(d2[2:], along_second(-1))
    own4, d1, d2 = lax.optimization_barrier((own4, d1, d2))
    others = [send(v, to_other_core) for v in (own4, d1, d2)]
    d3, d4, far_a, back_b, ahead_b = lax.optimization_barrier((d3, d4, far_a, back_b, ahead_b))
    far_b = send(back_b, along_x(1))
    others += [send(v, to_other_core) for v in (d3, d4)]
    cands = [own4, d1, d2, d3, d4, *others]
    blocks = [refs_a, refs_b, back_a, back_b, ahead_a, ahead_b, far_a, far_b]
    payload = score_pairs(pos, count, [*cands, *blocks])
    got = lax.all_to_all(payload, AXES, 0, 0)
    scores, totals = pl.pallas_call(
        finish_kernel,
        out_shape=[
            jax.ShapeDtypeStruct((3, 1, 1, SLOTS), jnp.float32),
            jax.ShapeDtypeStruct((1, 3), jnp.float32),
        ],
        name="finish",
    )(got)
    return scores, totals.reshape(3)


def solution(mesh):
    placed = (
        P("prompt", "dp", None, None),
        P("dp", "prompt", None, None),
        P("prompt", "dp", None),
        P("dp", "prompt", None),
        P("prompt", "dp"),
        P("dp", "prompt"),
        P(),
        P(),
        P(),
        P(),
        P(),
        P(),
        P(),
        P("dp", "prompt", None),
        P("dp", "prompt", None),
        P("dp", "prompt"),
    )
    return jax.shard_map(
        on_device,
        mesh=mesh,
        in_specs=placed,
        out_specs=(P(None, "dp", "prompt", None), P()),
        check_vma=False,
    )
```
